256 devices in a mesh: wide: 16 (over x, y), narrow: 16 (over z, core).
Axes of the slice: x: 4, y: 4, z: 8, core: 2. Of those that a mesh axis runs over, the one named last changes fastest.
Arguments:
- field: float32 [11, 384, 512, 128], P(None, 'wide', 'narrow'), may hold values from -110 to 110, as said below
- start_x: float32 [384, 64], replicated, may hold values from -0.3125 to 0.3125
- start_y: float32 [512, 64], replicated, may hold values from -0.25 to 0.25
- start_z: float32 [128, 64], replicated, may hold values from -0.5 to 0.5
Outputs:
- core_block: float32 [11, 64, 64, 64], P(None, 'narrow', 'wide')
- factor_x: float32 [384, 64], replicated
- factor_y: float32 [512, 64], replicated
- factor_z: float32 [128, 64], replicated
The draws below stay inside these ranges and needn't reach their ends.
Inputs may be any that keep to these rules, and one draw needn't show every extreme that they name: Real-valued field.
All inputs are finite; a program needn't handle non-finite values.
Results may differ from the reference program's by a relative error of at most 0.00024.
Values sent between devices are 32-bit elements; how exact they have to be, the bound alone decides.
A program may use at most 128 MiB of HBM per device.

```python
import jax
import jax.numpy as jnp
from jax import lax

S = 11
X = 384
Y = 512
Z = 128
R = 64
ITERS = 2


def scale_vector(key, count, low_end, high_end):
    return jnp.exp(jax.random.uniform(key, (count,), jnp.float32, jnp.log(low_end), jnp.log(high_end)))


def draw_field(key, part):
    keys = jax.random.split(jax.random.fold_in(key, 17), 9)
    noise = jax.random.truncated_normal(keys[0], -4.0, 4.0, (S, X, Y, Z), jnp.float32)
    low_end = 0.6
    high_end = 1.8
    scale_s = scale_vector(keys[1], S, low_end, high_end)
    scale_x = scale_vector(keys[2], X, low_end, high_end)
    scale_y = scale_vector(keys[3], Y, low_end, high_end)
    scale_z = scale_vector(keys[4], Z, low_end, high_end)
    scaled = noise * scale_s[:, None, None, None] * scale_x[None, :, None, None]
    scaled = scaled * scale_y[None, None, :, None] * scale_z[None, None, None, :]
    fac_s = jax.random.truncated_normal(keys[5], -4.0, 4.0, (8, S), jnp.float32)
    fac_x = jax.random.truncated_normal(keys[6], -4.0, 4.0, (8, X), jnp.float32)
    fac_y = jax.random.truncated_normal(keys[7], -4.0, 4.0, (8, Y), jnp.float32)
    fac_z = jax.random.truncated_normal(keys[8], -4.0, 4.0, (8, Z), jnp.float32)
    shared = 0.03 * jnp.einsum('ks,kx,ky,kz->sxyz', fac_s, fac_x, fac_y, fac_z)
    return (scaled + shared).astype(jnp.float32)


def gaussian(stream_key, dims, width, bound, held_as=jnp.bfloat16):
    drawn = width * jax.random.normal(stream_key, dims, jnp.float32)
    return jnp.clip(drawn, min=-bound, max=bound).astype(held_as)


def setup_inputs(seed: int = 0) -> dict:
    key_list = jax.random.split(jax.random.key(seed), 5)
    field = draw_field(jax.random.fold_in(key_list[4], 71), 0)
    start_x = gaussian(key_list[1], (X, R), X ** -0.5, 0.3125, jnp.float32)
    start_y = gaussian(key_list[2], (Y, R), Y ** -0.5, 0.25, jnp.float32)
    start_z = gaussian(key_list[3], (Z, R), Z ** -0.5, 0.5, jnp.float32)
    return dict(field=field, start_x=start_x, start_y=start_y, start_z=start_z)


def gram_ref(tensor, contracted):

    def one_species(species_slab):
        return lax.dot_general(species_slab, species_slab, ((contracted, contracted), ((), ())), precision=lax.Precision.HIGHEST)
    return jnp.sum(lax.map(one_species, tensor), axis=0)

def subspace(gram_full, start_cols):
    basis_now = start_cols
    for step_index in range(ITERS):
        image_cols = jnp.dot(gram_full, basis_now, precision=lax.Precision.HIGHEST)
        inner_prod = jnp.dot(image_cols.T, image_cols, precision=lax.Precision.HIGHEST)
        lower_tri = jnp.linalg.cholesky(inner_prod)
        basis_now = jax.scipy.linalg.solve_triangular(lower_tri, image_cols.T, lower=True).T
    return basis_now

def reference(field, start_x, start_y, start_z):
    factor_x = subspace(gram_ref(field, (1, 2)), start_x)
    core_x = jnp.einsum('sxyz,xr->sryz', field, factor_x, precision=lax.Precision.HIGHEST)
    factor_y = subspace(gram_ref(core_x, (0, 2)), start_y)
    core_y = jnp.einsum('sxyz,yr->sxrz', core_x, factor_y, precision=lax.Precision.HIGHEST)
    factor_z = subspace(gram_ref(core_y, (0, 1)), start_z)
    core_block = jnp.einsum('sxyz,zr->sxyr', core_y, factor_z, precision=lax.Precision.HIGHEST)
    return (core_block, factor_x, factor_y, factor_z)
```

```python
import functools

import jax
import jax.numpy as jnp
from jax import lax
from jax.experimental import pallas as pl
from jax.experimental.pallas import tpu as pltpu
from jax.sharding import PartitionSpec as P

ITERS = 2
MESH = pl.DeviceIdType.MESH
HIGH = lax.Precision.HIGHEST
F32 = jnp.float32
BF16 = jnp.bfloat16

S, X, Y, Z, R = 11, 384, 512, 128, 64
WX, WY = 4, 4
NW, NN = 16, 16
XB = X // NW
J = 3
NT = (((1,), (1,)), ((), ()))
TN = (((0,), (0,)), ((), ()))


def dot(a, b, dims=(((1,), (0,)), ((), ())), precision=None):
    return lax.dot_general(a, b, dims, precision=precision, preferred_element_type=F32)


def split(v):
    high = v.astype(BF16)
    return high, (v - high.astype(F32)).astype(BF16)


def pairs(size):
    blocks = size // 128
    return [(i, j) for i in range(blocks) for j in range(i, blocks)]


def block(i):
    return slice(i * 128, (i + 1) * 128)


def kernel(
    field, start_x, start_y, start_z,
    core_out, out_x, out_y, out_z,
    fibres, fib_hi, fib_lo, acc_hh, acc_hl,
    shrunk, columns, col_hi, col_lo, second, regrouped,
    part_x, arrive_x, own_x, near_x, mid_x, full_x,
    part_y, arrive_y, own_y, near_y, mid_y, full_y,
    part_z, arrive_z, own_z, near_z, mid_z, full_z,
    gram, basis, elim,
    send_a, recv_a, local_a,
    send_c, recv_c, local_c,
    send_d, recv_d, local_d,
    send_g, recv_g,
):
    w = lax.axis_index("wide")
    n = lax.axis_index("narrow")
    wx, wy = w // WY, w % WY

    barrier = pltpu.get_barrier_semaphore()

    def greet(wide, narrow):
        pl.semaphore_signal(barrier, inc=1, device_id=(wide, narrow), device_id_type=MESH)

    @pl.loop(1, NW)
    def _(d):
        greet((w + d) % NW, n)
        greet(w, (n + d) % NN)

    @pl.loop(1, WY)
    def _(dy):
        @pl.loop(1, NN)
        def _(dn):
            greet(wx * WY + (wy + dy) % WY, (n + dn) % NN)

    pl.semaphore_wait(barrier, 2 * (NW - 1) + (WY - 1) * (NN - 1))

    def remote(src, dst, send, recv, wide, narrow):
        return pltpu.make_async_remote_copy(
            src_ref=src, dst_ref=dst, send_sem=send, recv_sem=recv,
            device_id=(wide, narrow), device_id_type=MESH,
        )

    def await_recv(ref, sem):
        remote(ref, ref, sem, sem, w, n).wait_recv()

    def await_send(ref, sem):
        remote(ref, ref, sem, sem, w, n).wait_send()

    mine = pl.ds(w * XB, XB)

    for j in range(J):
        @pl.loop(1, NW)
        def _(d, j=j):
            t = (w + d) % NW
            species = t // WY + WX * j

            @pl.when(species < S)
            def _():
                remote(
                    field.at[species, :, t % WY], fibres.at[j, mine],
                    send_a, recv_a.at[j], t, n,
                ).start()

        @pl.when(wx + WX * j < S)
        def _(j=j):
            pltpu.make_async_copy(
                field.at[wx + WX * j, :, wy], fibres.at[j, mine], local_a.at[j]
            ).start()

    for j in range(J):
        @pl.when(wx + WX * j < S)
        def _(j=j):
            pltpu.make_async_copy(
                field.at[wx + WX * j, :, wy], fibres.at[j, mine], local_a.at[j]
            ).wait()
            await_recv(fibres.at[j, pl.ds(0, (NW - 1) * XB)], recv_a.at[j])

        @pl.when(wx + WX * j >= S)
        def _(j=j):
            fibres[j] = jnp.zeros(fibres.shape[1:], F32)

        lines = fibres.at[j].reshape(X * 8, Z)
        for y in range(8):
            high, low = split(lines[pl.ds(y, X, stride=8), :])
            fib_hi[j, :, block(y)] = high
            fib_lo[j, :, block(y)] = low
        high = fib_hi[j]
        hh = dot(high, high, NT)
        hl = dot(high, fib_lo[j], NT)
        acc_hh[:X, :X] = hh if j == 0 else acc_hh[:X, :X] + hh
        acc_hl[:X, :X] = hl if j == 0 else acc_hl[:X, :X] + hl

    def pack(size, part):
        for b, (i, j) in enumerate(pairs(size)):
            part[block(b), :] = (
                acc_hh[block(i), block(j)] + acc_hl[block(i), block(j)]
                + acc_hl[block(j), block(i)].T
            )

    def unpack(size, full):
        for b, (i, j) in enumerate(pairs(size)):
            one = full[block(b), :]
            gram[block(i), block(j)] = one
            if i != j:
                gram[block(j), block(i)] = one.T

    def all_reduce(mode, tiles, part, arrive, own, near, mid, full):
        rows = tiles * 8

        def share(which):
            return pl.ds(pl.multiple_of(which * rows, 8), rows)

        send = send_g.at[mode]

        @pl.loop(1, NW)
        def _(d):
            t = (w + d) % NW
            remote(part.at[share(t)], arrive.at[share(w)], send.at[0], recv_g.at[mode, 0], t, n).start()

        arrive[share(w), :] = part[share(w), :]
        await_recv(arrive.at[pl.ds(0, (NW - 1) * rows)], recv_g.at[mode, 0])
        total = arrive[pl.ds(0, rows), :]
        for t in range(1, NW):
            total = total + arrive[pl.ds(t * rows, rows), :]
        if tiles == 1:
            own[...] = total

            @pl.loop(1, NN)
            def _(d):
                t = (n + d) % NN
                remote(own, near.at[n], send.at[1], recv_g.at[mode, 1], w, t).start()

            near[n] = total
            await_recv(near.at[pl.ds(0, NN - 1)], recv_g.at[mode, 1])
            total = near[0]
            for t in range(1, NN):
                total = total + near[t]
            mid[0] = total
            await_send(near.at[pl.ds(0, NN - 1)], send.at[1])
        else:
            for t in range(tiles):
                own[t] = total[t * 8 : (t + 1) * 8]

            @pl.loop(0, tiles)
            def _(t):
                @pl.when(t != n)
                def _():
                    remote(own.at[t], near.at[n], send.at[1], recv_g.at[mode, 1], w, t).start()

            @pl.when(n < tiles)
            def _():
                near[n] = own[n]
                await_recv(near.at[pl.ds(0, NN - 1)], recv_g.at[mode, 1])
                final = near[0]
                for t in range(1, NN):
                    final = final + near[t]
                mid[n] = final

                @pl.loop(1, NN)
                def _(d):
                    t = (n + d) % NN
                    remote(mid.at[n], mid.at[n], send.at[2], recv_g.at[mode, 2], w, t).start()

                await_recv(mid.at[pl.ds(0, tiles - 1)], recv_g.at[mode, 2])
                await_send(near.at[pl.ds(0, NN - 1)], send.at[2])
                await_send(near.at[pl.ds(0, tiles - 1)], send.at[1])

            @pl.when(n >= tiles)
            def _():
                await_recv(mid.at[pl.ds(0, tiles)], recv_g.at[mode, 2])
                await_send(near.at[pl.ds(0, tiles)], send.at[1])

        @pl.loop(1, NW)
        def _(d):
            t = (w + d) % NW
            remote(mid, full.at[w], send.at[3], recv_g.at[mode, 3], t, n).start()

        full[w] = mid[...]
        await_recv(full.at[pl.ds(0, NW - 1)], recv_g.at[mode, 3])
        await_send(full.at[pl.ds(0, NW - 1)], send.at[3])
        await_send(arrive.at[pl.ds(0, (NW - 1) * rows)], send.at[0])

    row_of = lax.broadcasted_iota(jnp.int32, (R, 128), 0)
    line_of = lax.broadcasted_iota(jnp.int32, (8, 128), 0)

    def lower_inverse(inner):
        here = lax.broadcasted_iota(jnp.int32, (R, R), 0)
        there = lax.broadcasted_iota(jnp.int32, (R, R), 1)
        elim[:, :R] = inner
        elim[:, R:] = (here == there).astype(F32)

        def step(b, _):
            start = pl.multiple_of(b * 8, 8)
            whole = elim[...]
            panel = elim[pl.ds(start, 8), :]
            below = row_of >= (b + 1) * 8
            for i in range(8):
                row = panel[i : i + 1, :]
                scale = lax.rsqrt(row[:, i : i + 1])
                row = row * scale
                panel = jnp.where(
                    line_of == i, jnp.broadcast_to(row, (8, 128)),
                    panel - jnp.where(line_of > i, panel[:, i : i + 1] * scale, 0.0) * row,
                )
                whole = whole - jnp.where(below, whole[:, i : i + 1] * scale, 0.0) * row
            elim[...] = pltpu.roll(whole, 120, 1)
            elim[pl.ds(start, 8), :] = pltpu.roll(panel, 120, 1)
            return 0

        lax.fori_loop(0, R // 8, step, 0)
        return elim[:, :R]

    def subspace(size, start, out):
        basis[:size, :] = start[...]

        def turn(_, carry):
            image = dot(gram[:size, :size], basis[:size, :], precision=HIGH)
            inner = dot(image, image, TN, HIGH)
            basis[:size, :] = dot(image, lower_inverse(inner), NT, HIGH)
            return carry

        lax.fori_loop(0, ITERS, turn, 0)
        out[...] = basis[:size, :]

    pack(X, part_x)
    all_reduce(0, 6, part_x, arrive_x, own_x, near_x, mid_x, full_x)
    unpack(X, full_x.reshape(6 * 128, 128))
    subspace(X, start_x, out_x)

    high, low = split(basis[:X, :].T)
    slab = wx * WY
    for j in range(J):
        part = dot(high, fib_hi[j]) + dot(high, fib_lo[j]) + dot(low, fib_hi[j])
        lines = shrunk.at[j].reshape(R * 8, Z)
        for y in range(8):
            lines[pl.ds(y, R, stride=8), :] = part[:, block(y)]

        @pl.when(wx + WX * j < S)
        def _(j=j):
            @pl.loop(1, R)
            def _(d):
                t = (n * WY + wy + d) % R
                remote(
                    shrunk.at[j, t], columns.at[j, n * WY + wy], send_c, recv_c.at[j],
                    slab + t % WY, t // WY,
                ).start()

            columns[j, n * WY + wy] = shrunk[j, n * WY + wy]

    for j in range(J):
        @pl.when(wx + WX * j < S)
        def _(j=j):
            await_recv(columns.at[j, pl.ds(0, R - 1)], recv_c.at[j])

        @pl.when(wx + WX * j >= S)
        def _(j=j):
            columns[j] = jnp.zeros(columns.shape[1:], F32)

        high, low = split(columns[j].reshape(Y, Z))
        col_hi[:, block(j)] = high
        col_lo[:, block(j)] = low
    high = col_hi[...]
    acc_hh[...] = dot(high, high, NT)
    acc_hl[...] = dot(high, col_lo[...], NT)
    pack(Y, part_y)
    all_reduce(1, 10, part_y, arrive_y, own_y, near_y, mid_y, full_y)
    unpack(Y, full_y.reshape(10 * 128, 128))
    subspace(Y, start_y, out_y)

    row = lax.broadcasted_iota(jnp.int32, (2 * R, R), 0)
    col = lax.broadcasted_iota(jnp.int32, (2 * R, R), 1)
    spread = ((row % 8 < 4) & (row // 8 * 4 + row % 8 == col)).astype(F32)
    high, low = split(dot(spread, basis[:Y, :], NT, HIGH))
    part = dot(high, col_hi[...]) + dot(high, col_lo[...]) + dot(low, col_hi[...])
    total = jnp.zeros((Z, Z), F32)
    for j in range(J):
        one = part[:, block(j)]
        second[j] = one.reshape(NW, 8, Z)
        total = total + dot(one, one, TN, HIGH)
    part_z[...] = total

    @pl.loop(1, NW)
    def _(d):
        t = (w + d) % NW
        remote(second.at[:, t], regrouped.at[:, w], send_d, recv_d, t, n).start()

    for j in range(J):
        regrouped[j, w] = second[j, w]
    all_reduce(2, 1, part_z, arrive_z, own_z, near_z, mid_z, full_z)
    gram[:Z, :Z] = full_z[...].reshape(Z, Z)
    subspace(Z, start_z, out_z)

    await_recv(regrouped.at[:, pl.ds(0, NW - 1)], recv_d)
    core_out[...] = dot(regrouped[...].reshape(J * NW * 8, Z), basis[:Z, :], precision=HIGH)

    await_send(regrouped.at[:, pl.ds(0, NW - 1)], send_d)
    for j in range(J):
        @pl.when(wx + WX * j < S)
        def _(j=j):
            await_send(columns.at[j, pl.ds(0, R - 1)], send_c)
    for j in range(J - 1):
        await_send(fibres.at[j, pl.ds(0, (NW - 1) * XB)], send_a)
    last = WY * (S - WX * (J - 1))

    @pl.when(wx + WX * (J - 1) < S)
    def _():
        await_send(fibres.at[J - 1, pl.ds(0, (last - 1) * XB)], send_a)

    @pl.when(wx + WX * (J - 1) >= S)
    def _():
        await_send(fibres.at[J - 1, pl.ds(0, last * XB)], send_a)


def reduce_scratch(tiles):
    rows = tiles * 128
    return [
        pltpu.VMEM((rows, 128), F32),
        pltpu.VMEM((rows, 128), F32),
        pltpu.VMEM((tiles, 8, 128) if tiles > 1 else (8, 128), F32),
        pltpu.VMEM((NN, 8, 128), F32),
        pltpu.VMEM((tiles, 8, 128), F32),
        pltpu.VMEM((NW, tiles, 8, 128), F32),
    ]


def body(field, start_x, start_y, start_z):
    vmem = pl.BlockSpec(memory_space=pltpu.VMEM)
    dma = pltpu.SemaphoreType.DMA
    core, fx, fy, fz = pl.pallas_call(
        kernel,
        out_shape=(
            jax.ShapeDtypeStruct((J * NW * 8, R), F32),
            jax.ShapeDtypeStruct((X, R), F32),
            jax.ShapeDtypeStruct((Y, R), F32),
            jax.ShapeDtypeStruct((Z, R), F32),
        ),
        in_specs=[pl.BlockSpec(memory_space=pl.ANY), vmem, vmem, vmem],
        out_specs=(vmem,) * 4,
        scratch_shapes=[
            pltpu.VMEM((J, X, 8, Z), F32),
            pltpu.VMEM((J, X, 8 * Z), BF16),
            pltpu.VMEM((J, X, 8 * Z), BF16),
            pltpu.VMEM((Y, Y), F32),
            pltpu.VMEM((Y, Y), F32),
            pltpu.VMEM((J, R, 8, Z), F32),
            pltpu.VMEM((J, R, 8, Z), F32),
            pltpu.VMEM((Y, J * Z), BF16),
            pltpu.VMEM((Y, J * Z), BF16),
            pltpu.VMEM((J, NW, 8, Z), F32),
            pltpu.VMEM((J, NW, 8, Z), F32),
            *reduce_scratch(6),
            *reduce_scratch(10),
            *reduce_scratch(1),
            pltpu.VMEM((Y, Y), F32),
            pltpu.VMEM((Y, R), F32),
            pltpu.VMEM((R, 128), F32),
            dma, dma((J,)), dma((J,)),
            dma, dma((J,)), dma,
            dma, dma, dma,
            dma((3, 4)), dma((3, 4)),
        ],
        compiler_params=pltpu.CompilerParams(collective_id=0, has_side_effects=True),
    )(field.reshape(S, XB, WY, 8, Z), start_x, start_y, start_z)
    core = core.reshape(WX * J, NN // 4, 8, R)[:S, :, :4, :]
    return core, fx, fy, fz


def solution(mesh):
    return jax.shard_map(
        body,
        mesh=mesh,
        in_specs=(P(None, "wide", "narrow", None), P(), P(), P()),
        out_specs=(P(None, "narrow", "wide", None), P(), P(), P()),
        check_vma=False,
    )
```

```python
import functools

import jax
import jax.numpy as jnp
from jax import lax
from jax.experimental import pallas as pl
from jax.experimental.pallas import tpu as pltpu
from jax.sharding import PartitionSpec as P

ITERS = 2
MESH = pl.DeviceIdType.MESH
HIGH = lax.Precision.HIGHEST
F32 = jnp.float32
BF16 = jnp.bfloat16

S, X, Y, Z, R = 11, 384, 512, 128, 64
WX, WY = 4, 4
NW, NN = 16, 16
XB = X // NW
PARTS = 3
J = 3
NT = (((1,), (1,)), ((), ()))
TN = (((0,), (0,)), ((), ()))


def dot(a, b, dims=(((1,), (0,)), ((), ())), precision=None):
    return lax.dot_general(a, b, dims, precision=precision, preferred_element_type=F32)


def split(v):
    high = v.astype(BF16)
    return high, (v - high.astype(F32)).astype(BF16)


def pairs(size):
    blocks = size // 128
    return [(i, j) for i in range(blocks) for j in range(i, blocks)]


def block(i):
    return slice(i * 128, (i + 1) * 128)


def kernel(
    field, start_x, start_y, start_z,
    core_out, out_x, out_y, out_z,
    fibres, fib_hi, fib_lo, acc_hh, acc_hl,
    shrunk, columns, col_hi, col_lo, second, regrouped,
    part_x, arrive_x, own_x, near_x, mid_x, full_x,
    part_y, arrive_y, own_y, near_y, mid_y, full_y,
    part_z, arrive_z, own_z, near_z, mid_z, full_z,
    gram, begin_x, begin_y, begin_z, basis_x, basis_y, basis_z, elim,
    load_s,
    send_a, recv_a, local_a,
    send_c, recv_c, local_c,
    send_d, recv_d, local_d,
    send_g, recv_g,
):
    w = lax.axis_index("wide")
    n = lax.axis_index("narrow")
    wx, wy = lax.div(w, WY), lax.rem(w, WY)
    nz, nc = lax.div(n, 2), lax.rem(n, 2)
    at_x = [lax.rem(wx + d, WX) for d in range(WX)]
    at_y = [lax.rem(wy + d, WY) for d in range(WY)]
    starts = [
        pltpu.make_async_copy(source, target, load_s.at[i])
        for i, (source, target) in enumerate(
            ((start_x, begin_x), (start_y, begin_y), (start_z, begin_z))
        )
    ]
    for one in starts:
        one.start()

    barrier = pltpu.get_barrier_semaphore()

    def greet(wide, narrow):
        pl.semaphore_signal(barrier, inc=1, device_id=(wide, narrow), device_id_type=MESH)

    @pl.loop(1, NW)
    def _(d):
        greet((w + d) % NW, n)
        greet(w, (n + d) % NN)

    @pl.loop(1, WY)
    def _(dy):
        @pl.loop(1, NN)
        def _(dn):
            greet(wx * WY + (wy + dy) % WY, (n + dn) % NN)

    pl.semaphore_wait(barrier, 2 * (NW - 1) + (WY - 1) * (NN - 1))

    def remote(src, dst, send, recv, wide, narrow):
        return pltpu.make_async_remote_copy(
            src_ref=src, dst_ref=dst, send_sem=send, recv_sem=recv,
            device_id=(wide, narrow), device_id_type=MESH,
        )

    def await_recv(ref, sem):
        remote(ref, ref, sem, sem, w, n).wait_recv()

    def await_send(ref, sem):
        remote(ref, ref, sem, sem, w, n).wait_send()

    mine = pl.ds(w * XB, XB)

    def send_lines(j):
        @pl.loop(0, PARTS)
        def _(q):
            for dx in range(WX):
                for dy in range(WY):
                    if dx or dy:
                        def one(dx=dx, dy=dy):
                            rows = pl.ds(q * (XB // PARTS), XB // PARTS)
                            there = pl.ds(w * XB + q * (XB // PARTS), XB // PARTS)
                            remote(
                                field.at[at_x[dx] + WX * j, rows, at_y[dy]], fibres.at[j, there],
                                send_a, recv_a.at[j], at_x[dx] * WY + at_y[dy], n,
                            ).start()

                        if WX * (j + 1) <= S:
                            one()
                        else:
                            pl.when(at_x[dx] + WX * j < S)(one)

    for j in range(J):
        send_lines(j)

        @pl.when(wx + WX * j < S)
        def _(j=j):
            pltpu.make_async_copy(
                field.at[wx + WX * j, :, wy], fibres.at[j, mine], local_a.at[j]
            ).start()

    for j in range(J):
        @pl.when(wx + WX * j < S)
        def _(j=j):
            pltpu.make_async_copy(
                field.at[wx + WX * j, :, wy], fibres.at[j, mine], local_a.at[j]
            ).wait()
            await_recv(fibres.at[j, pl.ds(0, (NW - 1) * XB)], recv_a.at[j])

        @pl.when(wx + WX * j >= S)
        def _(j=j):
            fibres[j] = jnp.zeros(fibres.shape[1:], F32)

        lines = fibres.at[j].reshape(X * 8, Z)
        for y in range(8):
            high, low = split(lines[pl.ds(y, X, stride=8), :])
            fib_hi[j, :, block(y)] = high
            fib_lo[j, :, block(y)] = low
        high = fib_hi[j]
        hh = dot(high, high, NT)
        hl = dot(high, fib_lo[j], NT)
        acc_hh[:X, :X] = hh if j == 0 else acc_hh[:X, :X] + hh
        acc_hl[:X, :X] = hl if j == 0 else acc_hl[:X, :X] + hl

    def pack(blocks, part):
        for b, (i, j) in enumerate(blocks):
            part[block(b), :] = (
                acc_hh[block(i), block(j)] + acc_hl[block(i), block(j)]
                + acc_hl[block(j), block(i)].T
            )

    def unpack(blocks, full):
        for b, (i, j) in enumerate(blocks):
            one = full[block(b), :]
            gram[block(i), block(j)] = one
            if i != j:
                gram[block(j), block(i)] = one.T

    def all_reduce(mode, size, chunks, tiles, part, arrive, own, near, mid, full):
        rows = tiles * 8
        blocks = pairs(size)

        def spread(chunk):
            if chunks > 1:
                pack(blocks[chunk * tiles :][:tiles], part.at[chunk].reshape(tiles * 128, 128))
            for dx in range(WX):
                for dy in range(WY):
                    if dx or dy:
                        t = at_x[dx] * WY + at_y[dy]
                        remote(
                            part.at[chunk, t], arrive.at[chunk, w],
                            send_g.at[mode, 0], recv_g.at[mode, 0, chunk], t, n,
                        ).start()

        def across(chunk):
            arrive[chunk, w] = part[chunk, w]
            await_recv(arrive.at[chunk, pl.ds(0, NW - 1)], recv_g.at[mode, 0, chunk])
            total = arrive[chunk, 0]
            for t in range(1, NW):
                total = total + arrive[chunk, t]
            own[chunk] = total.reshape(tiles, 8, 128)
            if chunks == 1:
                near[n] = own[0, 0]

                @pl.loop(1, NN)
                def _(d):
                    t = lax.rem(n + d, NN)
                    remote(own.at[0, 0], near.at[n], send_g.at[mode, 1], recv_g.at[mode, 1, 0], w, t).start()
            else:
                @pl.loop(0, tiles)
                def _(t):
                    @pl.when(t + chunk * tiles != n)
                    def _():
                        remote(
                            own.at[chunk, t], near.at[n], send_g.at[mode, 1],
                            recv_g.at[mode, 1, 0], w, t + chunk * tiles,
                        ).start()

        def add_near():
            total = near[0]
            for t in range(1, NN):
                total = total + near[t]
            return total

        def back(chunk):
            if chunks == 1:
                await_recv(near.at[pl.ds(0, NN - 1)], recv_g.at[mode, 1, 0])
                mid[0, 0] = add_near()
            else:
                first = chunk * tiles
                mine_now = (n >= first) & (n < first + tiles)
                tile = n - first

                @pl.when(mine_now)
                def _():
                    near[n] = own[chunk, tile]
                    await_recv(near.at[pl.ds(0, NN - 1)], recv_g.at[mode, 1, 0])
                    mid[chunk, tile] = add_near()

                    @pl.loop(1, NN)
                    def _(d):
                        t = lax.rem(n + d, NN)
                        remote(
                            mid.at[chunk, tile], mid.at[chunk, tile], send_g.at[mode, 2],
                            recv_g.at[mode, 2, chunk], w, t,
                        ).start()

        def share(chunk):
            if chunks > 1:
                first = chunk * tiles
                mine_now = (n >= first) & (n < first + tiles)

                @pl.when(mine_now)
                def _():
                    if tiles > 1:
                        await_recv(mid.at[chunk, pl.ds(0, tiles - 1)], recv_g.at[mode, 2, chunk])

                @pl.when(jnp.logical_not(mine_now))
                def _():
                    await_recv(mid.at[chunk], recv_g.at[mode, 2, chunk])

            for dx in range(WX):
                for dy in range(WY):
                    if dx or dy:
                        remote(
                            mid.at[chunk], full.at[chunk, w], send_g.at[mode, 3],
                            recv_g.at[mode, 3, chunk], at_x[dx] * WY + at_y[dy], n,
                        ).start()
            full[chunk, w] = mid[chunk]

        for stage in (spread, across, back, share):
            for chunk in range(chunks):
                stage(chunk)
        for chunk in range(chunks):
            await_recv(full.at[chunk, pl.ds(0, NW - 1)], recv_g.at[mode, 3, chunk])
            unpack(blocks[chunk * tiles :][:tiles], full.at[chunk].reshape(tiles * 128, 128))

        def drain():
            for chunk in range(chunks):
                await_send(full.at[chunk, pl.ds(0, NW - 1)], send_g.at[mode, 0])
                await_send(full.at[chunk, pl.ds(0, NW - 1)], send_g.at[mode, 3])
            count = chunks * tiles
            if chunks == 1:
                await_send(near.at[pl.ds(0, NN - 1)], send_g.at[mode, 1])
            else:
                @pl.when(n < count)
                def _():
                    await_send(near.at[pl.ds(0, NN - 1)], send_g.at[mode, 2])
                    await_send(near.at[pl.ds(0, count - 1)], send_g.at[mode, 1])

                @pl.when(n >= count)
                def _():
                    await_send(near.at[pl.ds(0, count)], send_g.at[mode, 1])

        return drain

    row_of = lax.broadcasted_iota(jnp.int32, (R, 128), 0)
    line_of = lax.broadcasted_iota(jnp.int32, (8, 128), 0)

    def lower_inverse(inner):
        here = lax.broadcasted_iota(jnp.int32, (R, R), 0)
        there = lax.broadcasted_iota(jnp.int32, (R, R), 1)
        elim[:, :R] = inner
        elim[:, R:] = (here == there).astype(F32)

        def step(b, _):
            start = pl.multiple_of(b * 8, 8)
            whole = elim[...]
            panel = elim[pl.ds(start, 8), :]
            below = row_of >= (b + 1) * 8
            heads = [jnp.broadcast_to(panel[:, i : i + 1], (8, 128)) for i in range(8)]
            lower = [jnp.where(below, whole[:, i : i + 1], 0.0) for i in range(8)]
            for i in range(8):
                scale = lax.rsqrt(heads[i][i : i + 1, :])
                row = panel[i : i + 1, :] * scale
                factor = jnp.where(line_of > i, heads[i] * scale, 0.0)
                under = lower[i] * scale
                for c in range(i + 1, 8):
                    pivot = heads[c][i : i + 1, :] * scale
                    heads[c] = heads[c] - factor * pivot
                    lower[c] = lower[c] - under * pivot
                panel = jnp.where(line_of == i, jnp.broadcast_to(row, (8, 128)), panel - factor * row)
                whole = whole - under * row
            elim[...] = pltpu.roll(whole, 120, 1)
            elim[pl.ds(start, 8), :] = pltpu.roll(panel, 120, 1)
            return 0

        lax.fori_loop(0, R // 8, step, 0)
        return elim[:, :R]

    def subspace(mode, size, begin, basis, out):
        starts[mode].wait()
        basis[...] = begin[...].T

        def turn(_, carry):
            image = dot(gram[:size, :size], basis[...], precision=HIGH)
            inner = dot(image, image, TN, HIGH)
            basis[...] = dot(image, lower_inverse(inner), NT, HIGH)
            return carry

        lax.fori_loop(0, ITERS, turn, 0)
        out[...] = basis[...].T

    drain_x = all_reduce(0, X, 2, 3, part_x, arrive_x, own_x, near_x, mid_x, full_x)
    subspace(0, X, begin_x, basis_x, out_x)

    high, low = split(out_x[...])
    slab = wx * WY
    for j in range(J):
        part = dot(high, fib_hi[j]) + dot(high, fib_lo[j]) + dot(low, fib_hi[j])
        lines = shrunk.at[j].reshape(R * 8, Z)
        for y in range(8):
            lines[pl.ds(y, R, stride=8), :] = part[:, block(y)]

        @pl.when(wx + WX * j < S)
        def _(j=j):
            @pl.loop(0, 8)
            def _(i):
                half = lax.div(i, 2)
                odd = lax.rem(i, 2)
                z = lax.rem(nz + 4 + half + odd - 2 * odd * (half + 1) + 8, 8)
                for dc in range(2):
                    for dy in range(WY):
                        def one(dc=dc, dy=dy):
                            core = lax.rem(nc + dc, 2)
                            t = z * 2 + core
                            remote(
                                shrunk.at[j, t * WY + at_y[dy]], columns.at[j, n * WY + wy], send_c,
                                recv_c.at[j], slab + at_y[dy], t,
                            ).start()

                        if dc or dy:
                            one()
                        else:
                            pl.when(z != nz)(one)

            columns[j, n * WY + wy] = shrunk[j, n * WY + wy]

    for j in range(J):
        @pl.when(wx + WX * j < S)
        def _(j=j):
            await_recv(columns.at[j, pl.ds(0, R - 1)], recv_c.at[j])

        @pl.when(wx + WX * j >= S)
        def _(j=j):
            columns[j] = jnp.zeros(columns.shape[1:], F32)

        high, low = split(columns[j].reshape(Y, Z))
        col_hi[:, block(j)] = high
        col_lo[:, block(j)] = low
    high = col_hi[...]
    acc_hh[...] = dot(high, high, NT)
    acc_hl[...] = dot(high, col_lo[...], NT)
    drain_y = all_reduce(1, Y, 2, 5, part_y, arrive_y, own_y, near_y, mid_y, full_y)
    subspace(1, Y, begin_y, basis_y, out_y)

    row = lax.broadcasted_iota(jnp.int32, (2 * R, R), 0)
    col = lax.broadcasted_iota(jnp.int32, (2 * R, R), 1)
    spread = ((row % 8 < 4) & (row // 8 * 4 + row % 8 == col)).astype(F32)
    high, low = split(dot(spread, out_y[...], precision=HIGH))
    part = dot(high, col_hi[...]) + dot(high, col_lo[...]) + dot(low, col_hi[...])
    total = jnp.zeros((Z, Z), F32)
    for j in range(J):
        one = part[:, block(j)]
        second[j] = one.reshape(NW, 8, Z)
        total = total + dot(one, one, TN, HIGH)
    part_z[...] = total.reshape(1, NW, 8, 128)

    @pl.loop(1, NW)
    def _(d):
        t = (w + d) % NW
        remote(second.at[:, t], regrouped.at[:, w], send_d, recv_d, t, n).start()

    for j in range(J):
        regrouped[j, w] = second[j, w]
    drain_z = all_reduce(2, Z, 1, 1, part_z, arrive_z, own_z, near_z, mid_z, full_z)
    subspace(2, Z, begin_z, basis_z, out_z)

    await_recv(regrouped.at[:, pl.ds(0, NW - 1)], recv_d)
    core_out[...] = dot(regrouped[...].reshape(J * NW * 8, Z), basis_z[...], precision=HIGH)

    drain_x()
    drain_y()
    drain_z()
    await_send(regrouped.at[:, pl.ds(0, NW - 1)], send_d)
    for j in range(J):
        @pl.when(wx + WX * j < S)
        def _(j=j):
            await_send(columns.at[j, pl.ds(0, R - 1)], send_c)
    for j in range(J - 1):
        await_send(fibres.at[j, pl.ds(0, (NW - 1) * XB)], send_a)
    last = WY * (S - WX * (J - 1))

    @pl.when(wx + WX * (J - 1) < S)
    def _():
        await_send(fibres.at[J - 1, pl.ds(0, (last - 1) * XB)], send_a)

    @pl.when(wx + WX * (J - 1) >= S)
    def _():
        await_send(fibres.at[J - 1, pl.ds(0, last * XB)], send_a)


def reduce_scratch(chunks, tiles):
    rows = tiles * 8
    return [
        pltpu.VMEM((chunks, NW, rows, 128), F32),
        pltpu.VMEM((chunks, NW, rows, 128), F32),
        pltpu.VMEM((chunks, tiles, 8, 128), F32),
        pltpu.VMEM((NN, 8, 128), F32),
        pltpu.VMEM((chunks, tiles, 8, 128), F32),
        pltpu.VMEM((chunks, NW, tiles, 8, 128), F32),
    ]


def hand_over(core, fx, fy, fz, core_out, out_x, out_y, out_z):
    core_out[...] = core[...].reshape(WX * J, NN // 4, 8, R)[:S, :, :4, :]
    out_x[...] = fx[...]
    out_y[...] = fy[...]
    out_z[...] = fz[...]


def finish(*arrays):
    vmem = pl.BlockSpec(memory_space=pltpu.VMEM)
    return pl.pallas_call(
        hand_over,
        out_shape=(
            jax.ShapeDtypeStruct((S, NN // 4, 4, R), F32),
            jax.ShapeDtypeStruct((R, X), F32),
            jax.ShapeDtypeStruct((R, Y), F32),
            jax.ShapeDtypeStruct((R, Z), F32),
        ),
        in_specs=[vmem] * 4,
    )(*arrays)


def body(field, start_x, start_y, start_z):
    vmem = pl.BlockSpec(memory_space=pltpu.VMEM)
    dma = pltpu.SemaphoreType.DMA
    core, fx, fy, fz = pl.pallas_call(
        kernel,
        out_shape=(
            jax.ShapeDtypeStruct((J * NW * 8, R), F32),
            jax.ShapeDtypeStruct((R, X), F32),
            jax.ShapeDtypeStruct((R, Y), F32),
            jax.ShapeDtypeStruct((R, Z), F32),
        ),
        in_specs=[pl.BlockSpec(memory_space=pl.ANY)] * 4,
        out_specs=(vmem,) * 4,
        scratch_shapes=[
            pltpu.VMEM((J, X, 8, Z), F32),
            pltpu.VMEM((J, X, 8 * Z), BF16),
            pltpu.VMEM((J, X, 8 * Z), BF16),
            pltpu.VMEM((Y, Y), F32),
            pltpu.VMEM((Y, Y), F32),
            pltpu.VMEM((J, R, 8, Z), F32),
            pltpu.VMEM((J, R, 8, Z), F32),
            pltpu.VMEM((Y, J * Z), BF16),
            pltpu.VMEM((Y, J * Z), BF16),
            pltpu.VMEM((J, NW, 8, Z), F32),
            pltpu.VMEM((J, NW, 8, Z), F32),
            *reduce_scratch(2, 3),
            *reduce_scratch(2, 5),
            *reduce_scratch(1, 1),
            pltpu.VMEM((Y, Y), F32),
            pltpu.VMEM((R, X), F32),
            pltpu.VMEM((R, Y), F32),
            pltpu.VMEM((R, Z), F32),
            pltpu.VMEM((X, R), F32),
            pltpu.VMEM((Y, R), F32),
            pltpu.VMEM((Z, R), F32),
            pltpu.VMEM((R, 128), F32),
            dma((3,)),
            dma, dma((J,)), dma((J,)),
            dma, dma((J,)), dma,
            dma, dma, dma,
            dma((3, 4)), dma((3, 4, 2)),
        ],
        compiler_params=pltpu.CompilerParams(collective_id=0, has_side_effects=True),
    )(field.reshape(S, XB, WY, 8, Z), start_x.T, start_y.T, start_z.T)
    core, fx, fy, fz = finish(core, fx, fy, fz)
    return core, fx.T, fy.T, fz.T


def solution(mesh):
    return jax.shard_map(
        body,
        mesh=mesh,
        in_specs=(P(None, "wide", "narrow", None), P(), P(), P()),
        out_specs=(P(None, "narrow", "wide", None), P(), P(), P()),
        check_vma=False,
    )
```

```python
import functools

import jax
import jax.numpy as jnp
from jax import lax
from jax.experimental import pallas as pl
from jax.experimental.pallas import tpu as pltpu
from jax.sharding import PartitionSpec as P

ITERS = 2
MESH = pl.DeviceIdType.MESH
HIGH = lax.Precision.HIGHEST
F32 = jnp.float32
BF16 = jnp.bfloat16

S, X, Y, Z, R = 11, 384, 512, 128, 64
WX, WY = 4, 4
NW, NN = 16, 16
XB = X // NW
PARTS = 3
J = 3
NT = (((1,), (1,)), ((), ()))
TN = (((0,), (0,)), ((), ()))


def dot(a, b, dims=(((1,), (0,)), ((), ())), precision=None):
    return lax.dot_general(a, b, dims, precision=precision, preferred_element_type=F32)


def split(v):
    high = v.astype(BF16)
    return high, (v - high.astype(F32)).astype(BF16)


def pairs(size):
    blocks = size // 128
    return [(i, j) for i in range(blocks) for j in range(i, blocks)]


def block(i):
    return slice(i * 128, (i + 1) * 128)


def kernel(
    field, start_x, start_y, start_z,
    core_out, out_x, out_y, out_z,
    fibres, fib_hi, fib_lo, acc_hh, acc_hl,
    shrunk, columns, col_hi, col_lo, second, regrouped,
    part_x, pair_x, arrive_x, own_x, near_x, mid_x, full_x,
    part_y, pair_y, arrive_y, own_y, near_y, mid_y, full_y,
    part_z, arrive_z, own_z, near_z, mid_z, full_z,
    gram, begin_x, begin_y, begin_z, basis_x, basis_y, basis_z, elim,
    load_s,
    send_a, recv_a, local_a,
    send_c, recv_c, local_c,
    send_d, recv_d, local_d,
    send_g, recv_g,
):
    w = lax.axis_index("wide")
    n = lax.axis_index("narrow")
    wx, wy = lax.div(w, WY), lax.rem(w, WY)
    nz, nc = lax.div(n, 2), lax.rem(n, 2)
    at_x = [lax.rem(wx + d, WX) for d in range(WX)]
    at_y = [lax.rem(wy + d, WY) for d in range(WY)]
    starts = [
        pltpu.make_async_copy(source, target, load_s.at[i])
        for i, (source, target) in enumerate(
            ((start_x, begin_x), (start_y, begin_y), (start_z, begin_z))
        )
    ]
    for one in starts:
        one.start()

    barrier = pltpu.get_barrier_semaphore()

    def greet(wide, narrow):
        pl.semaphore_signal(barrier, inc=1, device_id=(wide, narrow), device_id_type=MESH)

    @pl.loop(1, NW)
    def _(d):
        greet((w + d) % NW, n)
        greet(w, (n + d) % NN)

    @pl.loop(1, WY)
    def _(dy):
        @pl.loop(1, NN)
        def _(dn):
            greet(wx * WY + (wy + dy) % WY, (n + dn) % NN)

    pl.semaphore_wait(barrier, 2 * (NW - 1) + (WY - 1) * (NN - 1))

    def remote(src, dst, send, recv, wide, narrow):
        return pltpu.make_async_remote_copy(
            src_ref=src, dst_ref=dst, send_sem=send, recv_sem=recv,
            device_id=(wide, narrow), device_id_type=MESH,
        )

    def await_recv(ref, sem):
        remote(ref, ref, sem, sem, w, n).wait_recv()

    def await_send(ref, sem):
        remote(ref, ref, sem, sem, w, n).wait_send()

    mine = pl.ds(w * XB, XB)

    def send_lines(j):
        @pl.loop(0, PARTS)
        def _(q):
            for dx in range(WX):
                for dy in range(WY):
                    if dx or dy:
                        def one(dx=dx, dy=dy):
                            rows = pl.ds(q * (XB // PARTS), XB // PARTS)
                            there = pl.ds(w * XB + q * (XB // PARTS), XB // PARTS)
                            remote(
                                field.at[at_x[dx] + WX * j, rows, at_y[dy]], fibres.at[j, there],
                                send_a, recv_a.at[j], at_x[dx] * WY + at_y[dy], n,
                            ).start()

                        if WX * (j + 1) <= S:
                            one()
                        else:
                            pl.when(at_x[dx] + WX * j < S)(one)

    for j in range(J):
        send_lines(j)

        @pl.when(wx + WX * j < S)
        def _(j=j):
            pltpu.make_async_copy(
                field.at[wx + WX * j, :, wy], fibres.at[j, mine], local_a.at[j]
            ).start()

    for j in range(J):
        @pl.when(wx + WX * j < S)
        def _(j=j):
            pltpu.make_async_copy(
                field.at[wx + WX * j, :, wy], fibres.at[j, mine], local_a.at[j]
            ).wait()
            await_recv(fibres.at[j, pl.ds(0, (NW - 1) * XB)], recv_a.at[j])

        @pl.when(wx + WX * j >= S)
        def _(j=j):
            fibres[j] = jnp.zeros(fibres.shape[1:], F32)

        lines = fibres.at[j].reshape(X * 8, Z)
        for y in range(8):
            high, low = split(lines[pl.ds(y, X, stride=8), :])
            fib_hi[j, :, block(y)] = high
            fib_lo[j, :, block(y)] = low
        high = fib_hi[j]
        hh = dot(high, high, NT)
        hl = dot(high, fib_lo[j], NT)
        acc_hh[:X, :X] = hh if j == 0 else acc_hh[:X, :X] + hh
        acc_hl[:X, :X] = hl if j == 0 else acc_hl[:X, :X] + hl

    def pack(i, j):
        return (
            acc_hh[block(i), block(j)] + acc_hl[block(i), block(j)]
            + acc_hl[block(j), block(i)].T
        ).reshape(NW, 8, 128)

    def unpack(i, j, one):
        one = one.reshape(128, 128)
        gram[block(i), block(j)] = one
        if i != j:
            gram[block(j), block(i)] = one.T

    def to_wide(source, target, send, recv):
        for dx in range(WX):
            for dy in range(WY):
                if dx or dy:
                    t = at_x[dx] * WY + at_y[dy]
                    remote(source(t), target, send, recv, t, n).start()

    partner = nz * 2 + 1 - nc

    def all_reduce(mode, size, cuts, part, pair, arrive, own, near, mid, full):
        places = pairs(size)
        half = len(places) // 2
        chunks = [(a, b - a) for a, b in zip((0, *cuts), (*cuts, half))]
        sends = [send_g.at[mode, stage] for stage in range(5)]

        def swap(c, first, count):
            for h in range(2):
                for k in range(first, first + count):
                    part[h, k] = pack(*places[h * half + k])
            here = pl.ds(first, count)
            remote(part.at[1 - nc, here], pair.at[here], sends[0], recv_g.at[mode, 0, c], w, partner).start()

        def spread(c, first, count):
            here = pl.ds(first, count)
            await_recv(pair.at[here], recv_g.at[mode, 0, c])
            pair[here] = part[nc, here] + pair[here]
            to_wide(lambda t: pair.at[here, t], arrive.at[here, w], sends[1], recv_g.at[mode, 1, c])
            arrive[here, w] = pair[here, w]

        def across(c, first, count):
            here = pl.ds(first, count)
            await_recv(arrive.at[here, pl.ds(0, NW - 1)], recv_g.at[mode, 1, c])
            total = arrive[here, 0]
            for t in range(1, NW):
                total = total + arrive[here, t]
            own[here] = total
            for d in (1, 7, 2, 6, 3, 5, 4):
                t = lax.rem(nz + d, 8) * 2 + nc
                remote(own.at[here], near.at[nz, here], sends[2], recv_g.at[mode, 2, c], w, t).start()
            near[nz, here] = total

        def back(c, first, count):
            here = pl.ds(first, count)
            await_recv(near.at[pl.ds(0, 7), here], recv_g.at[mode, 2, c])
            total = near[0, here]
            for t in range(1, 8):
                total = total + near[t, here]
            mid[here] = total
            to_wide(lambda t: mid.at[here], full.at[nc, here, w], sends[3], recv_g.at[mode, 3, c])
            full[nc, here, w] = total

        def share(c, first, count):
            here = pl.ds(first, count)
            await_recv(full.at[nc, here, pl.ds(0, NW - 1)], recv_g.at[mode, 3, c])
            remote(full.at[nc, here], full.at[nc, here], sends[4], recv_g.at[mode, 4, c], w, partner).start()

        def finish(c, first, count):
            here = pl.ds(first, count)
            await_recv(full.at[1 - nc, here], recv_g.at[mode, 4, c])
            for h in range(2):
                for k in range(first, first + count):
                    unpack(*places[h * half + k], full[h, k])

        for stage in (swap, spread, across, back, share, finish):
            for c, chunk in enumerate(chunks):
                stage(c, *chunk)

        def drain():
            await_send(pair, sends[0])
            await_send(arrive.at[:, pl.ds(0, NW - 1)], sends[1])
            await_send(near.at[pl.ds(0, 7)], sends[2])
            await_send(arrive.at[:, pl.ds(0, NW - 1)], sends[3])
            await_send(pair, sends[4])

        return drain

    def all_reduce_small(mode, part, arrive, own, near, mid, full):
        to_wide(lambda t: part.at[t], arrive.at[w], send_g.at[mode, 0], recv_g.at[mode, 0, 0])
        arrive[w] = part[w]
        await_recv(arrive.at[pl.ds(0, NW - 1)], recv_g.at[mode, 0, 0])
        total = arrive[0]
        for t in range(1, NW):
            total = total + arrive[t]
        own[...] = total
        for d in (2, 15, 3, 14, 4, 13, 5, 12, 6, 11, 7, 10, 8, 9, 1):
            t = lax.rem(n + d, NN)
            remote(own, near.at[n], send_g.at[mode, 1], recv_g.at[mode, 1, 0], w, t).start()
        near[n] = total
        await_recv(near.at[pl.ds(0, NN - 1)], recv_g.at[mode, 1, 0])
        total = near[0]
        for t in range(1, NN):
            total = total + near[t]
        mid[...] = total
        to_wide(lambda t: mid, full.at[w], send_g.at[mode, 2], recv_g.at[mode, 2, 0])
        full[w] = total
        await_recv(full.at[pl.ds(0, NW - 1)], recv_g.at[mode, 2, 0])

        def drain():
            for stage in range(3):
                await_send(full.at[pl.ds(0, NW - 1)], send_g.at[mode, stage])

        return drain

    row_of = lax.broadcasted_iota(jnp.int32, (R, 128), 0)
    line_of = lax.broadcasted_iota(jnp.int32, (8, 128), 0)

    def lower_inverse(inner):
        here = lax.broadcasted_iota(jnp.int32, (R, R), 0)
        there = lax.broadcasted_iota(jnp.int32, (R, R), 1)
        elim[:, :R] = inner
        elim[:, R:] = (here == there).astype(F32)

        def step(b, _):
            start = pl.multiple_of(b * 8, 8)
            whole = elim[...]
            panel = elim[pl.ds(start, 8), :]
            below = row_of >= (b + 1) * 8
            heads = [jnp.broadcast_to(panel[:, i : i + 1], (8, 128)) for i in range(8)]
            lower = [jnp.where(below, whole[:, i : i + 1], 0.0) for i in range(8)]
            for i in range(8):
                scale = lax.rsqrt(heads[i][i : i + 1, :])
                row = panel[i : i + 1, :] * scale
                factor = jnp.where(line_of > i, heads[i] * scale, 0.0)
                under = lower[i] * scale
                for c in range(i + 1, 8):
                    pivot = heads[c][i : i + 1, :] * scale
                    heads[c] = heads[c] - factor * pivot
                    lower[c] = lower[c] - under * pivot
                panel = jnp.where(line_of == i, jnp.broadcast_to(row, (8, 128)), panel - factor * row)
                whole = whole - under * row
            elim[...] = pltpu.roll(whole, 120, 1)
            elim[pl.ds(start, 8), :] = pltpu.roll(panel, 120, 1)
            return 0

        lax.fori_loop(0, R // 8, step, 0)
        return elim[:, :R]

    def subspace(mode, size, begin, basis, out):
        starts[mode].wait()
        basis[...] = begin[...].T

        def turn(_, carry):
            image = dot(gram[:size, :size], basis[...], precision=HIGH)
            inner = dot(image, image, TN, HIGH)
            basis[...] = dot(image, lower_inverse(inner), NT, HIGH)
            return carry

        lax.fori_loop(0, ITERS, turn, 0)
        out[...] = basis[...].T

    drain_x = all_reduce(0, X, (2,), part_x, pair_x, arrive_x, own_x, near_x, mid_x, full_x)
    subspace(0, X, begin_x, basis_x, out_x)

    high, low = split(out_x[...])
    slab = wx * WY
    for j in range(J):
        part = dot(high, fib_hi[j]) + dot(high, fib_lo[j]) + dot(low, fib_hi[j])
        lines = shrunk.at[j].reshape(R * 8, Z)
        for y in range(8):
            lines[pl.ds(y, R, stride=8), :] = part[:, block(y)]

        @pl.when(wx + WX * j < S)
        def _(j=j):
            @pl.loop(0, 8)
            def _(i):
                half = lax.div(i, 2)
                odd = lax.rem(i, 2)
                z = lax.rem(nz + 4 + half + odd - 2 * odd * (half + 1) + 8, 8)
                for dc in range(2):
                    for dy in range(WY):
                        def one(dc=dc, dy=dy):
                            core = lax.rem(nc + dc, 2)
                            t = z * 2 + core
                            remote(
                                shrunk.at[j, t * WY + at_y[dy]], columns.at[j, n * WY + wy], send_c,
                                recv_c.at[j], slab + at_y[dy], t,
                            ).start()

                        if dc or dy:
                            one()
                        else:
                            pl.when(z != nz)(one)

            columns[j, n * WY + wy] = shrunk[j, n * WY + wy]

    for j in range(J):
        @pl.when(wx + WX * j < S)
        def _(j=j):
            await_recv(columns.at[j, pl.ds(0, R - 1)], recv_c.at[j])

        @pl.when(wx + WX * j >= S)
        def _(j=j):
            columns[j] = jnp.zeros(columns.shape[1:], F32)

        high, low = split(columns[j].reshape(Y, Z))
        col_hi[:, block(j)] = high
        col_lo[:, block(j)] = low
    high = col_hi[...]
    acc_hh[...] = dot(high, high, NT)
    acc_hl[...] = dot(high, col_lo[...], NT)
    drain_y = all_reduce(1, Y, (3,), part_y, pair_y, arrive_y, own_y, near_y, mid_y, full_y)
    subspace(1, Y, begin_y, basis_y, out_y)

    row = lax.broadcasted_iota(jnp.int32, (2 * R, R), 0)
    col = lax.broadcasted_iota(jnp.int32, (2 * R, R), 1)
    spread = ((row % 8 < 4) & (row // 8 * 4 + row % 8 == col)).astype(F32)
    high, low = split(dot(spread, out_y[...], precision=HIGH))
    part = dot(high, col_hi[...]) + dot(high, col_lo[...]) + dot(low, col_hi[...])
    total = jnp.zeros((Z, Z), F32)
    for j in range(J):
        one = part[:, block(j)]
        second[j] = one.reshape(NW, 8, Z)
        total = total + dot(one, one, TN, HIGH)
    part_z[...] = total.reshape(NW, 8, 128)

    @pl.loop(1, NW)
    def _(d):
        t = (w + d) % NW
        remote(second.at[:, t], regrouped.at[:, w], send_d, recv_d, t, n).start()

    for j in range(J):
        regrouped[j, w] = second[j, w]
    drain_z = all_reduce_small(2, part_z, arrive_z, own_z, near_z, mid_z, full_z)
    gram[:Z, :Z] = full_z[...].reshape(Z, Z)
    subspace(2, Z, begin_z, basis_z, out_z)

    await_recv(regrouped.at[:, pl.ds(0, NW - 1)], recv_d)
    core_out[...] = dot(regrouped[...].reshape(J * NW * 8, Z), basis_z[...], precision=HIGH)

    drain_x()
    drain_y()
    drain_z()
    await_send(regrouped.at[:, pl.ds(0, NW - 1)], send_d)
    for j in range(J):
        @pl.when(wx + WX * j < S)
        def _(j=j):
            await_send(columns.at[j, pl.ds(0, R - 1)], send_c)
    for j in range(J - 1):
        await_send(fibres.at[j, pl.ds(0, (NW - 1) * XB)], send_a)
    last = WY * (S - WX * (J - 1))

    @pl.when(wx + WX * (J - 1) < S)
    def _():
        await_send(fibres.at[J - 1, pl.ds(0, (last - 1) * XB)], send_a)

    @pl.when(wx + WX * (J - 1) >= S)
    def _():
        await_send(fibres.at[J - 1, pl.ds(0, last * XB)], send_a)


def reduce_scratch(half):
    return [
        pltpu.VMEM((2, half, NW, 8, 128), F32),
        pltpu.VMEM((half, NW, 8, 128), F32),
        pltpu.VMEM((half, NW, 8, 128), F32),
        pltpu.VMEM((half, 8, 128), F32),
        pltpu.VMEM((8, half, 8, 128), F32),
        pltpu.VMEM((half, 8, 128), F32),
        pltpu.VMEM((2, half, NW, 8, 128), F32),
    ]


def hand_over(core, fx, fy, fz, core_out, out_x, out_y, out_z):
    core_out[...] = core[...].reshape(WX * J, NN // 4, 8, R)[:S, :, :4, :]
    out_x[...] = fx[...]
    out_y[...] = fy[...]
    out_z[...] = fz[...]


def finish(*arrays):
    vmem = pl.BlockSpec(memory_space=pltpu.VMEM)
    return pl.pallas_call(
        hand_over,
        out_shape=(
            jax.ShapeDtypeStruct((S, NN // 4, 4, R), F32),
            jax.ShapeDtypeStruct((R, X), F32),
            jax.ShapeDtypeStruct((R, Y), F32),
            jax.ShapeDtypeStruct((R, Z), F32),
        ),
        in_specs=[vmem] * 4,
    )(*arrays)


def body(field, start_x, start_y, start_z):
    vmem = pl.BlockSpec(memory_space=pltpu.VMEM)
    dma = pltpu.SemaphoreType.DMA
    core, fx, fy, fz = pl.pallas_call(
        kernel,
        out_shape=(
            jax.ShapeDtypeStruct((J * NW * 8, R), F32),
            jax.ShapeDtypeStruct((R, X), F32),
            jax.ShapeDtypeStruct((R, Y), F32),
            jax.ShapeDtypeStruct((R, Z), F32),
        ),
        in_specs=[pl.BlockSpec(memory_space=pl.ANY)] * 4,
        out_specs=(vmem,) * 4,
        scratch_shapes=[
            pltpu.VMEM((J, X, 8, Z), F32),
            pltpu.VMEM((J, X, 8 * Z), BF16),
            pltpu.VMEM((J, X, 8 * Z), BF16),
            pltpu.VMEM((Y, Y), F32),
            pltpu.VMEM((Y, Y), F32),
            pltpu.VMEM((J, R, 8, Z), F32),
            pltpu.VMEM((J, R, 8, Z), F32),
            pltpu.VMEM((Y, J * Z), BF16),
            pltpu.VMEM((Y, J * Z), BF16),
            pltpu.VMEM((J, NW, 8, Z), F32),
            pltpu.VMEM((J, NW, 8, Z), F32),
            *reduce_scratch(3),
            *reduce_scratch(5),
            pltpu.VMEM((NW, 8, 128), F32),
            pltpu.VMEM((NW, 8, 128), F32),
            pltpu.VMEM((8, 128), F32),
            pltpu.VMEM((NN, 8, 128), F32),
            pltpu.VMEM((8, 128), F32),
            pltpu.VMEM((NW, 8, 128), F32),
            pltpu.VMEM((Y, Y), F32),
            pltpu.VMEM((R, X), F32),
            pltpu.VMEM((R, Y), F32),
            pltpu.VMEM((R, Z), F32),
            pltpu.VMEM((X, R), F32),
            pltpu.VMEM((Y, R), F32),
            pltpu.VMEM((Z, R), F32),
            pltpu.VMEM((R, 128), F32),
            dma((3,)),
            dma, dma((J,)), dma((J,)),
            dma, dma((J,)), dma,
            dma, dma, dma,
            dma((3, 5)), dma((3, 5, 2)),
        ],
        compiler_params=pltpu.CompilerParams(collective_id=0, has_side_effects=True),
    )(field.reshape(S, XB, WY, 8, Z), start_x.T, start_y.T, start_z.T)
    core, fx, fy, fz = finish(core, fx, fy, fz)
    return core, fx.T, fy.T, fz.T


def solution(mesh):
    return jax.shard_map(
        body,
        mesh=mesh,
        in_specs=(P(None, "wide", "narrow", None), P(), P(), P()),
        out_specs=(P(None, "narrow", "wide", None), P(), P(), P()),
        check_vma=False,
    )
```

```python
import functools

import jax
import jax.numpy as jnp
from jax import lax
from jax.experimental import pallas as pl
from jax.experimental.pallas import tpu as pltpu
from jax.sharding import PartitionSpec as P

ITERS = 2
MESH = pl.DeviceIdType.MESH
HIGH = lax.Precision.HIGHEST
F32 = jnp.float32
BF16 = jnp.bfloat16

S, X, Y, Z, R = 11, 384, 512, 128, 64
WX, WY = 4, 4
NW, NN = 16, 16
XB = X // NW
PARTS = 3
J = 3
NT = (((1,), (1,)), ((), ()))
TN = (((0,), (0,)), ((), ()))


def dot(a, b, dims=(((1,), (0,)), ((), ())), precision=None):
    return lax.dot_general(a, b, dims, precision=precision, preferred_element_type=F32)


def split(v):
    high = v.astype(BF16)
    return high, (v - high.astype(F32)).astype(BF16)


def pairs(size):
    blocks = size // 128
    return [(i, j) for i in range(blocks) for j in range(i, blocks)]


def block(i):
    return slice(i * 128, (i + 1) * 128)


def kernel(
    field, start_x, start_y, start_z,
    core_out, out_x, out_y, out_z,
    fibres, fib_hi, fib_lo, acc_hh, acc_hl,
    shrunk, columns, col_hi, col_lo, second, regrouped,
    part_x, pair_x, arrive_x, own_x, near_x, mid_x, full_x,
    part_y, pair_y, arrive_y, own_y, near_y, mid_y, full_y,
    part_z, arrive_z, own_z, near_z, mid_z, full_z,
    gram, begin_x, begin_y, begin_z, elim,
    load_s,
    send_a, recv_a, local_a,
    send_c, recv_c, local_c,
    send_d, recv_d, local_d,
    send_g, recv_g,
):
    w = lax.axis_index("wide")
    n = lax.axis_index("narrow")
    wx, wy = lax.div(w, WY), lax.rem(w, WY)
    nz, nc = lax.div(n, 2), lax.rem(n, 2)
    at_x = [lax.rem(wx + d, WX) for d in range(WX)]
    at_y = [lax.rem(wy + d, WY) for d in range(WY)]
    starts = [
        pltpu.make_async_copy(source, target, load_s.at[i])
        for i, (source, target) in enumerate(
            ((start_x, begin_x), (start_y, begin_y), (start_z, begin_z))
        )
    ]
    for one in starts:
        one.start()

    barrier = pltpu.get_barrier_semaphore()

    def greet(wide, narrow):
        pl.semaphore_signal(barrier, inc=1, device_id=(wide, narrow), device_id_type=MESH)

    @pl.loop(1, NW)
    def _(d):
        greet(lax.rem(w + d, NW), n)
        greet(w, lax.rem(n + d, NN))

    pl.semaphore_wait(barrier, NW + NN - 2)

    def remote(src, dst, send, recv, wide, narrow):
        return pltpu.make_async_remote_copy(
            src_ref=src, dst_ref=dst, send_sem=send, recv_sem=recv,
            device_id=(wide, narrow), device_id_type=MESH,
        )

    def await_recv(ref, sem):
        remote(ref, ref, sem, sem, w, n).wait_recv()

    def await_send(ref, sem):
        remote(ref, ref, sem, sem, w, n).wait_send()

    mine = pl.ds(w * XB, XB)

    def send_lines(j):
        @pl.loop(0, PARTS)
        def _(q):
            for dx in range(WX):
                for dy in range(WY):
                    if dx or dy:
                        def one(dx=dx, dy=dy):
                            rows = pl.ds(q * (XB // PARTS), XB // PARTS)
                            there = pl.ds(w * XB + q * (XB // PARTS), XB // PARTS)
                            remote(
                                field.at[at_x[dx] + WX * j, rows, at_y[dy]], fibres.at[j, there],
                                send_a, recv_a.at[j], at_x[dx] * WY + at_y[dy], n,
                            ).start()

                        if WX * (j + 1) <= S:
                            one()
                        else:
                            pl.when(at_x[dx] + WX * j < S)(one)

    for j in range(J):
        send_lines(j)

        @pl.when(wx + WX * j < S)
        def _(j=j):
            pltpu.make_async_copy(
                field.at[wx + WX * j, :, wy], fibres.at[j, mine], local_a.at[j]
            ).start()

    for j in range(J):
        @pl.when(wx + WX * j < S)
        def _(j=j):
            pltpu.make_async_copy(
                field.at[wx + WX * j, :, wy], fibres.at[j, mine], local_a.at[j]
            ).wait()
            await_recv(fibres.at[j, pl.ds(0, (NW - 1) * XB)], recv_a.at[j])

        @pl.when(wx + WX * j >= S)
        def _(j=j):
            fibres[j] = jnp.zeros(fibres.shape[1:], F32)

        lines = fibres.at[j].reshape(X * 8, Z)
        for y in range(8):
            high, low = split(lines[pl.ds(y, X, stride=8), :])
            fib_hi[j, :, block(y)] = high
            fib_lo[j, :, block(y)] = low
        high = fib_hi[j]
        hh = dot(high, high, NT)
        hl = dot(high, fib_lo[j], NT)
        acc_hh[:X, :X] = hh if j == 0 else acc_hh[:X, :X] + hh
        acc_hl[:X, :X] = hl if j == 0 else acc_hl[:X, :X] + hl

    def pack(i, j):
        return (
            acc_hh[block(i), block(j)] + acc_hl[block(i), block(j)]
            + acc_hl[block(j), block(i)].T
        ).reshape(NW, 8, 128)

    def unpack(i, j, one):
        one = one.reshape(128, 128)
        gram[block(i), block(j)] = one
        if i != j:
            gram[block(j), block(i)] = one.T

    def to_wide(source, target, send, recv):
        for dx in range(WX):
            for dy in range(WY):
                if dx or dy:
                    t = at_x[dx] * WY + at_y[dy]
                    remote(source(t), target, send, recv, t, n).start()

    partner = nz * 2 + 1 - nc

    def all_reduce(mode, size, cuts, part, pair, arrive, own, near, mid, full):
        places = pairs(size)
        half = len(places) // 2
        chunks = [(a, b - a) for a, b in zip((0, *cuts), (*cuts, half))]
        sends = [send_g.at[mode, stage] for stage in range(5)]

        def swap(c, first, count):
            for h in range(2):
                for k in range(first, first + count):
                    part[h, k] = pack(*places[h * half + k])
            here = pl.ds(first, count)
            remote(part.at[1 - nc, here], pair.at[here], sends[0], recv_g.at[mode, 0, c], w, partner).start()

        def spread(c, first, count):
            here = pl.ds(first, count)
            await_recv(pair.at[here], recv_g.at[mode, 0, c])
            pair[here] = part[nc, here] + pair[here]
            to_wide(lambda t: pair.at[here, t], arrive.at[here, w], sends[1], recv_g.at[mode, 1, c])
            arrive[here, w] = pair[here, w]

        def across(c, first, count):
            here = pl.ds(first, count)
            await_recv(arrive.at[here, pl.ds(0, NW - 1)], recv_g.at[mode, 1, c])
            total = arrive[here, 0]
            for t in range(1, NW):
                total = total + arrive[here, t]
            own[here] = total
            for d in (1, 7, 2, 6, 3, 5, 4):
                t = lax.rem(nz + d, 8) * 2 + nc
                remote(own.at[here], near.at[nz, here], sends[2], recv_g.at[mode, 2, c], w, t).start()
            near[nz, here] = total

        def back(c, first, count):
            here = pl.ds(first, count)
            await_recv(near.at[pl.ds(0, 7), here], recv_g.at[mode, 2, c])
            total = near[0, here]
            for t in range(1, 8):
                total = total + near[t, here]
            mid[here] = total
            to_wide(lambda t: mid.at[here], full.at[nc, here, w], sends[3], recv_g.at[mode, 3, c])
            full[nc, here, w] = total

        def share(c, first, count):
            here = pl.ds(first, count)
            await_recv(full.at[nc, here, pl.ds(0, NW - 1)], recv_g.at[mode, 3, c])
            remote(full.at[nc, here], full.at[nc, here], sends[4], recv_g.at[mode, 4, c], w, partner).start()

        def finish(c, first, count):
            here = pl.ds(first, count)
            await_recv(full.at[1 - nc, here], recv_g.at[mode, 4, c])
            for h in range(2):
                for k in range(first, first + count):
                    unpack(*places[h * half + k], full[h, k])

        for stage in (swap, spread, across, back, share, finish):
            for c, chunk in enumerate(chunks):
                stage(c, *chunk)

        def drain():
            await_send(pair, sends[0])
            await_send(arrive.at[:, pl.ds(0, NW - 1)], sends[1])
            await_send(near.at[pl.ds(0, 7)], sends[2])
            await_send(arrive.at[:, pl.ds(0, NW - 1)], sends[3])
            await_send(pair, sends[4])

        return drain

    def all_reduce_small(mode, part, arrive, own, near, mid, full):
        to_wide(lambda t: part.at[t], arrive.at[w], send_g.at[mode, 0], recv_g.at[mode, 0, 0])
        arrive[w] = part[w]
        await_recv(arrive.at[pl.ds(0, NW - 1)], recv_g.at[mode, 0, 0])
        total = arrive[0]
        for t in range(1, NW):
            total = total + arrive[t]
        own[...] = total
        for d in (2, 15, 3, 14, 4, 13, 5, 12, 6, 11, 7, 10, 8, 9, 1):
            t = lax.rem(n + d, NN)
            remote(own, near.at[n], send_g.at[mode, 1], recv_g.at[mode, 1, 0], w, t).start()
        near[n] = total
        await_recv(near.at[pl.ds(0, NN - 1)], recv_g.at[mode, 1, 0])
        total = near[0]
        for t in range(1, NN):
            total = total + near[t]
        mid[...] = total
        to_wide(lambda t: mid, full.at[w], send_g.at[mode, 2], recv_g.at[mode, 2, 0])
        full[w] = total
        await_recv(full.at[pl.ds(0, NW - 1)], recv_g.at[mode, 2, 0])

        def drain():
            for stage in range(3):
                await_send(full.at[pl.ds(0, NW - 1)], send_g.at[mode, stage])

        return drain

    line_of = lax.broadcasted_iota(jnp.int32, (8, 128), 0)

    def lower_inverse(inner):
        here = lax.broadcasted_iota(jnp.int32, (R, R), 0)
        there = lax.broadcasted_iota(jnp.int32, (R, R), 1)
        elim[:, :R] = inner
        elim[:, R:] = (here == there).astype(F32)
        groups = [pl.ds(8 * g, 8) for g in range(R // 8)]
        for g, group in enumerate(groups):
            lanes = [slice(8 * g + i, 8 * g + i + 1) for i in range(8)]
            panel = elim[group, :]
            heads = [jnp.broadcast_to(panel[:, lane], (8, 128)) for lane in lanes]
            below = [elim[other, :] for other in groups[g + 1 :]]
            lower = [[jnp.broadcast_to(one[:, lane], (8, 128)) for lane in lanes] for one in below]
            for i in range(8):
                scale = lax.rsqrt(heads[i][i : i + 1, :])
                row = panel[i : i + 1, :] * scale
                factor = jnp.where(line_of > i, heads[i] * scale, 0.0)
                pivots = {c: heads[c][i : i + 1, :] * scale for c in range(i + 1, 8)}
                for c, pivot in pivots.items():
                    heads[c] = heads[c] - factor * pivot
                panel = jnp.where(line_of == i, jnp.broadcast_to(row, (8, 128)), panel - factor * row)
                for q in range(len(below)):
                    under = lower[q][i] * scale
                    for c, pivot in pivots.items():
                        lower[q][c] = lower[q][c] - under * pivot
                    below[q] = below[q] - under * row
            elim[group, :] = panel
            for other, one in zip(groups[g + 1 :], below):
                elim[other, :] = one
        return elim[:, R:]

    def subspace(mode, size, begin, basis):
        starts[mode].wait()
        basis[...] = begin[...]

        def turn(_, carry):
            image = dot(basis[...], gram[:size, :size], precision=HIGH)
            inner = dot(image, image, NT, HIGH)
            basis[...] = dot(lower_inverse(inner), image, precision=HIGH)
            return carry

        lax.fori_loop(0, ITERS, turn, 0)

    drain_x = all_reduce(0, X, (1,), part_x, pair_x, arrive_x, own_x, near_x, mid_x, full_x)
    subspace(0, X, begin_x, out_x)

    high, low = split(out_x[...])
    slab = wx * WY
    for j in range(J):
        part = dot(high, fib_hi[j]) + dot(high, fib_lo[j]) + dot(low, fib_hi[j])
        lines = shrunk.at[j].reshape(R * 8, Z)
        for y in range(8):
            lines[pl.ds(y, R, stride=8), :] = part[:, block(y)]

        @pl.when(wx + WX * j < S)
        def _(j=j):
            @pl.loop(0, 8)
            def _(i):
                half = lax.div(i, 2)
                odd = lax.rem(i, 2)
                z = lax.rem(nz + 4 + half + odd - 2 * odd * (half + 1) + 8, 8)
                for dc in range(2):
                    for dy in range(WY):
                        def one(dc=dc, dy=dy):
                            core = lax.rem(nc + dc, 2)
                            t = z * 2 + core
                            remote(
                                shrunk.at[j, t * WY + at_y[dy]], columns.at[j, n * WY + wy], send_c,
                                recv_c.at[j], slab + at_y[dy], t,
                            ).start()

                        if dc or dy:
                            one()
                        else:
                            pl.when(z != nz)(one)

            columns[j, n * WY + wy] = shrunk[j, n * WY + wy]

    for j in range(J):
        @pl.when(wx + WX * j < S)
        def _(j=j):
            await_recv(columns.at[j, pl.ds(0, R - 1)], recv_c.at[j])

        @pl.when(wx + WX * j >= S)
        def _(j=j):
            columns[j] = jnp.zeros(columns.shape[1:], F32)

        high, low = split(columns[j].reshape(Y, Z))
        col_hi[:, block(j)] = high
        col_lo[:, block(j)] = low
    high = col_hi[...]
    acc_hh[...] = dot(high, high, NT)
    acc_hl[...] = dot(high, col_lo[...], NT)
    drain_y = all_reduce(1, Y, (2,), part_y, pair_y, arrive_y, own_y, near_y, mid_y, full_y)
    subspace(1, Y, begin_y, out_y)

    row = lax.broadcasted_iota(jnp.int32, (2 * R, R), 0)
    col = lax.broadcasted_iota(jnp.int32, (2 * R, R), 1)
    spread = ((row % 8 < 4) & (row // 8 * 4 + row % 8 == col)).astype(F32)
    high, low = split(dot(spread, out_y[...], precision=HIGH))
    part = dot(high, col_hi[...]) + dot(high, col_lo[...]) + dot(low, col_hi[...])
    total = jnp.zeros((Z, Z), F32)
    for j in range(J):
        one = part[:, block(j)]
        second[j] = one.reshape(NW, 8, Z)
        total = total + dot(one, one, TN, HIGH)
    part_z[...] = total.reshape(NW, 8, 128)

    @pl.loop(1, NW)
    def _(d):
        t = (w + d) % NW
        remote(second.at[:, t], regrouped.at[:, w], send_d, recv_d, t, n).start()

    for j in range(J):
        regrouped[j, w] = second[j, w]
    drain_z = all_reduce_small(2, part_z, arrive_z, own_z, near_z, mid_z, full_z)
    gram[:Z, :Z] = full_z[...].reshape(Z, Z)
    subspace(2, Z, begin_z, out_z)

    await_recv(regrouped.at[:, pl.ds(0, NW - 1)], recv_d)
    core_out[...] = dot(regrouped[...].reshape(J * NW * 8, Z), out_z[...], NT, HIGH)

    drain_x()
    drain_y()
    drain_z()
    await_send(regrouped.at[:, pl.ds(0, NW - 1)], send_d)
    for j in range(J):
        @pl.when(wx + WX * j < S)
        def _(j=j):
            await_send(columns.at[j, pl.ds(0, R - 1)], send_c)
    for j in range(J - 1):
        await_send(fibres.at[j, pl.ds(0, (NW - 1) * XB)], send_a)
    last = WY * (S - WX * (J - 1))

    @pl.when(wx + WX * (J - 1) < S)
    def _():
        await_send(fibres.at[J - 1, pl.ds(0, (last - 1) * XB)], send_a)

    @pl.when(wx + WX * (J - 1) >= S)
    def _():
        await_send(fibres.at[J - 1, pl.ds(0, last * XB)], send_a)


def reduce_scratch(half):
    return [
        pltpu.VMEM((2, half, NW, 8, 128), F32),
        pltpu.VMEM((half, NW, 8, 128), F32),
        pltpu.VMEM((half, NW, 8, 128), F32),
        pltpu.VMEM((half, 8, 128), F32),
        pltpu.VMEM((8, half, 8, 128), F32),
        pltpu.VMEM((half, 8, 128), F32),
        pltpu.VMEM((2, half, NW, 8, 128), F32),
    ]


def hand_over(core, fx, fy, fz, core_out, out_x, out_y, out_z):
    core_out[...] = core[...].reshape(WX * J, NN // 4, 8, R)[:S, :, :4, :]
    out_x[...] = fx[...]
    out_y[...] = fy[...]
    out_z[...] = fz[...]


def finish(*arrays):
    vmem = pl.BlockSpec(memory_space=pltpu.VMEM)
    return pl.pallas_call(
        hand_over,
        out_shape=(
            jax.ShapeDtypeStruct((S, NN // 4, 4, R), F32),
            jax.ShapeDtypeStruct((R, X), F32),
            jax.ShapeDtypeStruct((R, Y), F32),
            jax.ShapeDtypeStruct((R, Z), F32),
        ),
        in_specs=[vmem] * 4,
    )(*arrays)


def body(field, start_x, start_y, start_z):
    vmem = pl.BlockSpec(memory_space=pltpu.VMEM)
    dma = pltpu.SemaphoreType.DMA
    core, fx, fy, fz = pl.pallas_call(
        kernel,
        out_shape=(
            jax.ShapeDtypeStruct((J * NW * 8, R), F32),
            jax.ShapeDtypeStruct((R, X), F32),
            jax.ShapeDtypeStruct((R, Y), F32),
            jax.ShapeDtypeStruct((R, Z), F32),
        ),
        in_specs=[pl.BlockSpec(memory_space=pl.ANY)] * 4,
        out_specs=(vmem,) * 4,
        scratch_shapes=[
            pltpu.VMEM((J, X, 8, Z), F32),
            pltpu.VMEM((J, X, 8 * Z), BF16),
            pltpu.VMEM((J, X, 8 * Z), BF16),
            pltpu.VMEM((Y, Y), F32),
            pltpu.VMEM((Y, Y), F32),
            pltpu.VMEM((J, R, 8, Z), F32),
            pltpu.VMEM((J, R, 8, Z), F32),
            pltpu.VMEM((Y, J * Z), BF16),
            pltpu.VMEM((Y, J * Z), BF16),
            pltpu.VMEM((J, NW, 8, Z), F32),
            pltpu.VMEM((J, NW, 8, Z), F32),
            *reduce_scratch(3),
            *reduce_scratch(5),
            pltpu.VMEM((NW, 8, 128), F32),
            pltpu.VMEM((NW, 8, 128), F32),
            pltpu.VMEM((8, 128), F32),
            pltpu.VMEM((NN, 8, 128), F32),
            pltpu.VMEM((8, 128), F32),
            pltpu.VMEM((NW, 8, 128), F32),
            pltpu.VMEM((Y, Y), F32),
            pltpu.VMEM((R, X), F32),
            pltpu.VMEM((R, Y), F32),
            pltpu.VMEM((R, Z), F32),
            pltpu.VMEM((R, 128), F32),
            dma((3,)),
            dma, dma((J,)), dma((J,)),
            dma, dma((J,)), dma,
            dma, dma, dma,
            dma((3, 5)), dma((3, 5, 2)),
        ],
        compiler_params=pltpu.CompilerParams(collective_id=0, has_side_effects=True),
    )(field.reshape(S, XB, WY, 8, Z), start_x.T, start_y.T, start_z.T)
    core, fx, fy, fz = finish(core, fx, fy, fz)
    return core, fx.T, fy.T, fz.T


def solution(mesh):
    return jax.shard_map(
        body,
        mesh=mesh,
        in_specs=(P(None, "wide", "narrow", None), P(), P(), P()),
        out_specs=(P(None, "narrow", "wide", None), P(), P(), P()),
        check_vma=False,
    )
```

```python
import functools

import jax
import jax.numpy as jnp
from jax import lax
from jax.experimental import pallas as pl
from jax.experimental.pallas import tpu as pltpu
from jax.sharding import PartitionSpec as P

ITERS = 2
MESH = pl.DeviceIdType.MESH
HIGH = lax.Precision.HIGHEST
F32 = jnp.float32
BF16 = jnp.bfloat16

S, X, Y, Z, R = 11, 384, 512, 128, 64
WX, WY = 4, 4
NW, NN = 16, 16
XB = X // NW
PARTS = 3
J = 3
NT = (((1,), (1,)), ((), ()))
TN = (((0,), (0,)), ((), ()))


def dot(a, b, dims=(((1,), (0,)), ((), ())), precision=None):
    return lax.dot_general(a, b, dims, precision=precision, preferred_element_type=F32)


def split(v):
    high = v.astype(BF16)
    return high, (v - high.astype(F32)).astype(BF16)


def pairs(size):
    blocks = size // 128
    return [(i, j) for i in range(blocks) for j in range(i, blocks)]


def block(i):
    return slice(i * 128, (i + 1) * 128)


def kernel(
    field, start_x, start_y, start_z,
    core_out, out_x, out_y, out_z,
    fibres, fib_hi, fib_lo, acc_hh, acc_hl,
    shrunk, columns, col_hi, col_lo, second, regrouped,
    part_x, pair_x, arrive_x, own_x, near_x, mid_x, full_x,
    part_y, pair_y, arrive_y, own_y, near_y, mid_y, full_y,
    part_z, arrive_z, own_z, near_z, mid_z, full_z,
    gram_hi, gram_lo, begin_x, begin_y, begin_z, elim,
    load_s, load_f, held,
    send_a, recv_a, local_a,
    send_c, recv_c, local_c,
    send_d, recv_d, local_d,
    send_g, recv_g,
):
    w = lax.axis_index("wide")
    n = lax.axis_index("narrow")
    wx, wy = lax.div(w, WY), lax.rem(w, WY)
    nz, nc = lax.div(n, 2), lax.rem(n, 2)
    at_x = [lax.rem(wx + d, WX) for d in range(WX)]
    at_y = [lax.rem(wy + d, WY) for d in range(WY)]
    starts = [
        pltpu.make_async_copy(source, target, load_s.at[i])
        for i, (source, target) in enumerate(
            ((start_x, begin_x), (start_y, begin_y), (start_z, begin_z))
        )
    ]
    for one in starts:
        one.start()

    stages = []
    for j in range(J):
        some = pl.ds(WX * j, min(WX, S - WX * j))
        stages.append(pltpu.make_async_copy(field.at[some], held.at[some], load_f.at[j]))
        stages[j].start()

    barrier = pltpu.get_barrier_semaphore()

    def greet(wide, narrow):
        pl.semaphore_signal(barrier, inc=1, device_id=(wide, narrow), device_id_type=MESH)

    @pl.loop(1, NW)
    def _(d):
        greet(lax.rem(w + d, NW), n)
        greet(w, lax.rem(n + d, NN))

    pl.semaphore_wait(barrier, NW + NN - 2)

    def remote(src, dst, send, recv, wide, narrow):
        return pltpu.make_async_remote_copy(
            src_ref=src, dst_ref=dst, send_sem=send, recv_sem=recv,
            device_id=(wide, narrow), device_id_type=MESH,
        )

    def await_recv(ref, sem):
        remote(ref, ref, sem, sem, w, n).wait_recv()

    def await_send(ref, sem):
        remote(ref, ref, sem, sem, w, n).wait_send()

    mine = pl.ds(w * XB, XB)

    def send_lines(j):
        @pl.loop(0, PARTS)
        def _(q):
            for dx in range(WX):
                for dy in range(WY):
                    if dx or dy:
                        def one(dx=dx, dy=dy):
                            rows = pl.ds(q * (XB // PARTS), XB // PARTS)
                            there = pl.ds(w * XB + q * (XB // PARTS), XB // PARTS)
                            remote(
                                held.at[at_x[dx] + WX * j, rows, at_y[dy]], fibres.at[j, there],
                                send_a, recv_a.at[j], at_x[dx] * WY + at_y[dy], n,
                            ).start()

                        if WX * (j + 1) <= S:
                            one()
                        else:
                            pl.when(at_x[dx] + WX * j < S)(one)

    for j in range(J):
        stages[j].wait()
        send_lines(j)

        @pl.when(wx + WX * j < S)
        def _(j=j):
            pltpu.make_async_copy(
                held.at[wx + WX * j, :, wy], fibres.at[j, mine], local_a.at[j]
            ).start()

    for j in range(J):
        @pl.when(wx + WX * j < S)
        def _(j=j):
            pltpu.make_async_copy(
                held.at[wx + WX * j, :, wy], fibres.at[j, mine], local_a.at[j]
            ).wait()
            await_recv(fibres.at[j, pl.ds(0, (NW - 1) * XB)], recv_a.at[j])

        @pl.when(wx + WX * j >= S)
        def _(j=j):
            fibres[j] = jnp.zeros(fibres.shape[1:], F32)

        lines = fibres.at[j].reshape(X * 8, Z)
        for y in range(8):
            high, low = split(lines[pl.ds(y, X, stride=8), :])
            fib_hi[j, :, block(y)] = high
            fib_lo[j, :, block(y)] = low
        high = fib_hi[j]
        hh = dot(high, high, NT)
        hl = dot(high, fib_lo[j], NT)
        acc_hh[:X, :X] = hh if j == 0 else acc_hh[:X, :X] + hh
        acc_hl[:X, :X] = hl if j == 0 else acc_hl[:X, :X] + hl

    def pack(i, j):
        return (
            acc_hh[block(i), block(j)] + acc_hl[block(i), block(j)]
            + acc_hl[block(j), block(i)].T
        ).reshape(NW, 8, 128)

    def unpack(i, j, one):
        one = one.reshape(128, 128)
        for here, there, values in ((i, j, one), (j, i, one.T))[: 1 + (i != j)]:
            gram_hi[block(here), block(there)], gram_lo[block(here), block(there)] = split(values)

    def to_wide(source, target, send, recv):
        for dx in range(WX):
            for dy in range(WY):
                if dx or dy:
                    t = at_x[dx] * WY + at_y[dy]
                    remote(source(t), target, send, recv, t, n).start()

    partner = nz * 2 + 1 - nc

    def all_reduce(mode, size, cuts, part, pair, arrive, own, near, mid, full):
        places = pairs(size)
        half = len(places) // 2
        chunks = [(a, b - a) for a, b in zip((0, *cuts), (*cuts, half))]
        sends = [send_g.at[mode, stage] for stage in range(5)]

        def swap(c, first, count):
            for h in range(2):
                for k in range(first, first + count):
                    part[h, k] = pack(*places[h * half + k])
            here = pl.ds(first, count)
            remote(part.at[1 - nc, here], pair.at[here], sends[0], recv_g.at[mode, 0, c], w, partner).start()

        def spread(c, first, count):
            here = pl.ds(first, count)
            await_recv(pair.at[here], recv_g.at[mode, 0, c])
            pair[here] = part[nc, here] + pair[here]
            to_wide(lambda t: pair.at[here, t], arrive.at[here, w], sends[1], recv_g.at[mode, 1, c])
            arrive[here, w] = pair[here, w]

        def across(c, first, count):
            here = pl.ds(first, count)
            await_recv(arrive.at[here, pl.ds(0, NW - 1)], recv_g.at[mode, 1, c])
            total = arrive[here, 0]
            for t in range(1, NW):
                total = total + arrive[here, t]
            own[here] = total
            for d in (1, 7, 2, 6, 3, 5, 4):
                t = lax.rem(nz + d, 8) * 2 + nc
                remote(own.at[here], near.at[nz, here], sends[2], recv_g.at[mode, 2, c], w, t).start()
            near[nz, here] = total

        def back(c, first, count):
            here = pl.ds(first, count)
            await_recv(near.at[pl.ds(0, 7), here], recv_g.at[mode, 2, c])
            total = near[0, here]
            for t in range(1, 8):
                total = total + near[t, here]
            mid[here] = total
            to_wide(lambda t: mid.at[here], full.at[nc, here, w], sends[3], recv_g.at[mode, 3, c])
            full[nc, here, w] = total

        def share(c, first, count):
            here = pl.ds(first, count)
            await_recv(full.at[nc, here, pl.ds(0, NW - 1)], recv_g.at[mode, 3, c])
            remote(full.at[nc, here], full.at[nc, here], sends[4], recv_g.at[mode, 4, c], w, partner).start()

        def finish(c, first, count):
            here = pl.ds(first, count)
            await_recv(full.at[1 - nc, here], recv_g.at[mode, 4, c])
            for h in range(2):
                for k in range(first, first + count):
                    unpack(*places[h * half + k], full[h, k])

        for stage in (swap, spread, across, back, share, finish):
            for c, chunk in enumerate(chunks):
                stage(c, *chunk)

        def drain():
            await_send(pair, sends[0])
            await_send(arrive.at[:, pl.ds(0, NW - 1)], sends[1])
            await_send(near.at[pl.ds(0, 7)], sends[2])
            await_send(arrive.at[:, pl.ds(0, NW - 1)], sends[3])
            await_send(pair, sends[4])

        return drain

    def all_reduce_small(mode, part, arrive, own, near, mid, full):
        to_wide(lambda t: part.at[t], arrive.at[w], send_g.at[mode, 0], recv_g.at[mode, 0, 0])
        arrive[w] = part[w]
        await_recv(arrive.at[pl.ds(0, NW - 1)], recv_g.at[mode, 0, 0])
        total = arrive[0]
        for t in range(1, NW):
            total = total + arrive[t]
        own[...] = total
        for d in (2, 15, 3, 14, 4, 13, 5, 12, 6, 11, 7, 10, 8, 9, 1):
            t = lax.rem(n + d, NN)
            remote(own, near.at[n], send_g.at[mode, 1], recv_g.at[mode, 1, 0], w, t).start()
        near[n] = total
        await_recv(near.at[pl.ds(0, NN - 1)], recv_g.at[mode, 1, 0])
        total = near[0]
        for t in range(1, NN):
            total = total + near[t]
        mid[...] = total
        to_wide(lambda t: mid, full.at[w], send_g.at[mode, 2], recv_g.at[mode, 2, 0])
        full[w] = total
        await_recv(full.at[pl.ds(0, NW - 1)], recv_g.at[mode, 2, 0])

        def drain():
            for stage in range(3):
                await_send(full.at[pl.ds(0, NW - 1)], send_g.at[mode, stage])

        return drain

    line_of = lax.broadcasted_iota(jnp.int32, (8, 128), 0)

    def lower_inverse(inner):
        here = lax.broadcasted_iota(jnp.int32, (R, R), 0)
        there = lax.broadcasted_iota(jnp.int32, (R, R), 1)
        elim[:, :R] = inner
        elim[:, R:] = (here == there).astype(F32)
        groups = [pl.ds(8 * g, 8) for g in range(R // 8)]
        for g, group in enumerate(groups):
            lanes = [slice(8 * g + i, 8 * g + i + 1) for i in range(8)]
            panel = elim[group, :]
            heads = [jnp.broadcast_to(panel[:, lane], (8, 128)) for lane in lanes]
            below = [elim[other, :] for other in groups[g + 1 :]]
            lower = [[jnp.broadcast_to(one[:, lane], (8, 128)) for lane in lanes] for one in below]
            for i in range(8):
                scale = lax.rsqrt(heads[i][i : i + 1, :])
                row = panel[i : i + 1, :] * scale
                factor = jnp.where(line_of > i, heads[i] * scale, 0.0)
                pivots = {c: heads[c][i : i + 1, :] * scale for c in range(i + 1, 8)}
                for c, pivot in pivots.items():
                    heads[c] = heads[c] - factor * pivot
                panel = jnp.where(line_of == i, jnp.broadcast_to(row, (8, 128)), panel - factor * row)
                for q in range(len(below)):
                    under = lower[q][i] * scale
                    for c, pivot in pivots.items():
                        lower[q][c] = lower[q][c] - under * pivot
                    below[q] = below[q] - under * row
            elim[group, :] = panel
            for other, one in zip(groups[g + 1 :], below):
                elim[other, :] = one
        return elim[:, R:]

    def subspace(mode, size, begin, basis):
        starts[mode].wait()
        basis[...] = begin[...]

        def turn(_, carry):
            high, low = split(basis[...])
            both = dot(jnp.concatenate([high, low], axis=0), gram_hi[:size, :size])
            image = both[:R] + both[R:] + dot(high, gram_lo[:size, :size])
            inner = dot(image, image, NT, HIGH)
            basis[...] = dot(lower_inverse(inner), image, precision=HIGH)
            return carry

        lax.fori_loop(0, ITERS, turn, 0)

    drain_x = all_reduce(0, X, (1,), part_x, pair_x, arrive_x, own_x, near_x, mid_x, full_x)
    subspace(0, X, begin_x, out_x)

    high, low = split(out_x[...])
    slab = wx * WY
    for j in range(J):
        part = dot(high, fib_hi[j]) + dot(high, fib_lo[j]) + dot(low, fib_hi[j])
        lines = shrunk.at[j].reshape(R * 8, Z)
        for y in range(8):
            lines[pl.ds(y, R, stride=8), :] = part[:, block(y)]

        @pl.when(wx + WX * j < S)
        def _(j=j):
            @pl.loop(0, 8)
            def _(i):
                half = lax.div(i, 2)
                odd = lax.rem(i, 2)
                z = lax.rem(nz + 4 + half + odd - 2 * odd * (half + 1) + 8, 8)
                for dc in range(2):
                    for dy in range(WY):
                        def one(dc=dc, dy=dy):
                            core = lax.rem(nc + dc, 2)
                            t = z * 2 + core
                            remote(
                                shrunk.at[j, t * WY + at_y[dy]], columns.at[j, n * WY + wy], send_c,
                                recv_c.at[j], slab + at_y[dy], t,
                            ).start()

                        if dc or dy:
                            one()
                        else:
                            pl.when(z != nz)(one)

            columns[j, n * WY + wy] = shrunk[j, n * WY + wy]

    for j in range(J):
        @pl.when(wx + WX * j < S)
        def _(j=j):
            await_recv(columns.at[j, pl.ds(0, R - 1)], recv_c.at[j])

        @pl.when(wx + WX * j >= S)
        def _(j=j):
            columns[j] = jnp.zeros(columns.shape[1:], F32)

        high, low = split(columns[j].reshape(Y, Z))
        col_hi[:, block(j)] = high
        col_lo[:, block(j)] = low
    high = col_hi[...]
    acc_hh[...] = dot(high, high, NT)
    acc_hl[...] = dot(high, col_lo[...], NT)
    drain_y = all_reduce(1, Y, (2,), part_y, pair_y, arrive_y, own_y, near_y, mid_y, full_y)
    subspace(1, Y, begin_y, out_y)

    row = lax.broadcasted_iota(jnp.int32, (2 * R, R), 0)
    col = lax.broadcasted_iota(jnp.int32, (2 * R, R), 1)
    spread = ((row % 8 < 4) & (row // 8 * 4 + row % 8 == col)).astype(F32)
    high, low = split(dot(spread, out_y[...], precision=HIGH))
    part = dot(high, col_hi[...]) + dot(high, col_lo[...]) + dot(low, col_hi[...])
    total = jnp.zeros((Z, Z), F32)
    for j in range(J):
        one = part[:, block(j)]
        second[j] = one.reshape(NW, 8, Z)
        total = total + dot(one, one, TN, HIGH)
    part_z[...] = total.reshape(NW, 8, 128)

    @pl.loop(1, NW)
    def _(d):
        t = (w + d) % NW
        remote(second.at[:, t], regrouped.at[:, w], send_d, recv_d, t, n).start()

    for j in range(J):
        regrouped[j, w] = second[j, w]
    drain_z = all_reduce_small(2, part_z, arrive_z, own_z, near_z, mid_z, full_z)
    unpack(0, 0, full_z[...])
    subspace(2, Z, begin_z, out_z)

    await_recv(regrouped.at[:, pl.ds(0, NW - 1)], recv_d)
    core_out[...] = dot(regrouped[...].reshape(J * NW * 8, Z), out_z[...], NT, HIGH)

    drain_x()
    drain_y()
    drain_z()
    await_send(regrouped.at[:, pl.ds(0, NW - 1)], send_d)
    for j in range(J):
        @pl.when(wx + WX * j < S)
        def _(j=j):
            await_send(columns.at[j, pl.ds(0, R - 1)], send_c)
    for j in range(J - 1):
        await_send(fibres.at[j, pl.ds(0, (NW - 1) * XB)], send_a)
    last = WY * (S - WX * (J - 1))

    @pl.when(wx + WX * (J - 1) < S)
    def _():
        await_send(fibres.at[J - 1, pl.ds(0, (last - 1) * XB)], send_a)

    @pl.when(wx + WX * (J - 1) >= S)
    def _():
        await_send(fibres.at[J - 1, pl.ds(0, last * XB)], send_a)


def reduce_scratch(half):
    return [
        pltpu.VMEM((2, half, NW, 8, 128), F32),
        pltpu.VMEM((half, NW, 8, 128), F32),
        pltpu.VMEM((half, NW, 8, 128), F32),
        pltpu.VMEM((half, 8, 128), F32),
        pltpu.VMEM((8, half, 8, 128), F32),
        pltpu.VMEM((half, 8, 128), F32),
        pltpu.VMEM((2, half, NW, 8, 128), F32),
    ]


def hand_over(core, fx, fy, fz, core_out, out_x, out_y, out_z):
    core_out[...] = core[...].reshape(WX * J, NN // 4, 8, R)[:S, :, :4, :]
    out_x[...] = fx[...]
    out_y[...] = fy[...]
    out_z[...] = fz[...]


def finish(*arrays):
    vmem = pl.BlockSpec(memory_space=pltpu.VMEM)
    return pl.pallas_call(
        hand_over,
        out_shape=(
            jax.ShapeDtypeStruct((S, NN // 4, 4, R), F32),
            jax.ShapeDtypeStruct((R, X), F32),
            jax.ShapeDtypeStruct((R, Y), F32),
            jax.ShapeDtypeStruct((R, Z), F32),
        ),
        in_specs=[vmem] * 4,
    )(*arrays)


def body(field, start_x, start_y, start_z):
    vmem = pl.BlockSpec(memory_space=pltpu.VMEM)
    dma = pltpu.SemaphoreType.DMA
    core, fx, fy, fz = pl.pallas_call(
        kernel,
        out_shape=(
            jax.ShapeDtypeStruct((J * NW * 8, R), F32),
            jax.ShapeDtypeStruct((R, X), F32),
            jax.ShapeDtypeStruct((R, Y), F32),
            jax.ShapeDtypeStruct((R, Z), F32),
        ),
        in_specs=[pl.BlockSpec(memory_space=pl.ANY)] * 4,
        out_specs=(vmem,) * 4,
        scratch_shapes=[
            pltpu.VMEM((J, X, 8, Z), F32),
            pltpu.VMEM((J, X, 8 * Z), BF16),
            pltpu.VMEM((J, X, 8 * Z), BF16),
            pltpu.VMEM((Y, Y), F32),
            pltpu.VMEM((Y, Y), F32),
            pltpu.VMEM((J, R, 8, Z), F32),
            pltpu.VMEM((J, R, 8, Z), F32),
            pltpu.VMEM((Y, J * Z), BF16),
            pltpu.VMEM((Y, J * Z), BF16),
            pltpu.VMEM((J, NW, 8, Z), F32),
            pltpu.VMEM((J, NW, 8, Z), F32),
            *reduce_scratch(3),
            *reduce_scratch(5),
            pltpu.VMEM((NW, 8, 128), F32),
            pltpu.VMEM((NW, 8, 128), F32),
            pltpu.VMEM((8, 128), F32),
            pltpu.VMEM((NN, 8, 128), F32),
            pltpu.VMEM((8, 128), F32),
            pltpu.VMEM((NW, 8, 128), F32),
            pltpu.VMEM((Y, Y), BF16),
            pltpu.VMEM((Y, Y), BF16),
            pltpu.VMEM((R, X), F32),
            pltpu.VMEM((R, Y), F32),
            pltpu.VMEM((R, Z), F32),
            pltpu.VMEM((R, 128), F32),
            dma((3,)),
            dma((J,)),
            pltpu.VMEM((S, XB, WY, 8, Z), F32),
            dma, dma((J,)), dma((J,)),
            dma, dma((J,)), dma,
            dma, dma, dma,
            dma((3, 5)), dma((3, 5, 2)),
        ],
        compiler_params=pltpu.CompilerParams(collective_id=0, has_side_effects=True),
    )(field.reshape(S, XB, WY, 8, Z), start_x.T, start_y.T, start_z.T)
    core, fx, fy, fz = finish(core, fx, fy, fz)
    return core, fx.T, fy.T, fz.T


def solution(mesh):
    return jax.shard_map(
        body,
        mesh=mesh,
        in_specs=(P(None, "wide", "narrow", None), P(), P(), P()),
        out_specs=(P(None, "narrow", "wide", None), P(), P(), P()),
        check_vma=False,
    )
```
